32 devices in a mesh: dp: 2 (over x), fsdp: 4 (over z), tensor: 4 (over y, core).
Axes of the slice: x: 2, y: 2, z: 4, core: 2. Of those that a mesh axis runs over, the one named last changes fastest.
Arguments:
- images: bfloat16 [16, 577, 1024], P(('dp', 'fsdp')), may hold values from -6 to 6
- cotangent: bfloat16 [16, 577, 1024], P(('dp', 'fsdp')), may hold values from -6 to 6
- qkv_weight: bfloat16 [2, 3, 1024, 1024], P(None, None, 'fsdp', 'tensor'), may hold values from -0.1875 to 0.1875
- out_weight: bfloat16 [2, 1024, 1024], P(None, 'tensor', 'fsdp'), may hold values from -3 to 3
- up_weight: bfloat16 [2, 1024, 4096], P(None, 'fsdp', 'tensor'), may hold values from -0.1875 to 0.1875
- down_weight: bfloat16 [2, 4096, 1024], P(None, 'tensor', 'fsdp'), may hold values from -0.09375 to 0.09375
- query_bias: bfloat16 [2, 16, 64], P(None, 'tensor', 'fsdp'), may hold values from -3 to 3
- value_bias: bfloat16 [2, 16, 64], P(None, 'tensor', 'fsdp'), may hold values from -0.19921875 to 0.19921875
- up_bias: bfloat16 [2, 16, 256], P(None, 'tensor', 'fsdp'), may hold values from -3 to 3
- norm_gain: bfloat16 [2, 2, 1024], P(None, None, 'fsdp'), may hold values from 0.5 to 1.5
- norm_shift: bfloat16 [2, 4, 1024], P(None, None, 'fsdp'), may hold values from -2 to 2
Outputs:
- out_images: bfloat16 [16, 577, 1024], P(('dp', 'fsdp'))
- grad_images: bfloat16 [16, 577, 1024], P(('dp', 'fsdp'))
- grad_qkv_weight: float32 [2, 3, 1024, 1024], P(None, None, 'fsdp', 'tensor')
- grad_out_weight: float32 [2, 1024, 1024], P(None, 'tensor', 'fsdp')
- grad_up_weight: float32 [2, 1024, 4096], P(None, 'fsdp', 'tensor')
- grad_down_weight: float32 [2, 4096, 1024], P(None, 'tensor', 'fsdp')
- grad_query_bias: float32 [2, 16, 64], P(None, 'tensor', 'fsdp')
- grad_value_bias: float32 [2, 16, 64], P(None, 'tensor', 'fsdp')
- grad_up_bias: float32 [2, 16, 256], P(None, 'tensor', 'fsdp')
- grad_norm_gain: float32 [2, 2, 1024], P(None, None, 'fsdp')
- grad_norm_shift: float32 [2, 4, 1024], P(None, None, 'fsdp')
The draws below stay inside these ranges and needn't reach their ends.
All inputs are finite; a program needn't handle non-finite values.
Results may differ from the reference program's by a relative error of at most 0.023.
Values may be sent and summed in bfloat16 or wider, within the bound.
A program may use at most 256 MiB of HBM per device.

```python
import math
import jax
import jax.numpy as jnp
from jax import lax

D = 1024
HEADS = 16
HD = 64
FF = 4096
SEQ = 577
LAYERS = 2
IMAGES = 16


def level_of(rng, dims, cuts, smallest, high):
    def one(position, blocks):
        heights = jax.random.uniform(jax.random.fold_in(jax.random.fold_in(rng, 6), position), (blocks,), jnp.float32, smallest / len(cuts), high / len(cuts))
        return jnp.repeat(jnp.exp(heights), dims[position] // blocks).reshape((-1,) + (1,) * (len(dims) - position - 1))

    level = one(*cuts[0])
    for cut in cuts[1:]:
        level = level * one(*cut)
    return level


def gaussian(key, extent, width, limit, pieces=(), dtype=jnp.bfloat16):
    entries = jax.random.normal(key, extent, jnp.float32) * width
    if len(pieces) > 0:
        entries = level_of(key, extent, pieces, -0.22, 0.18) * entries
    return jnp.clip(entries, min=-limit, max=limit).astype(dtype)


def setup_inputs(seed: int = 0) -> dict:
    keys = jax.random.split(jax.random.key(seed), 12)
    return {
        "images": gaussian(keys[0], (IMAGES, SEQ, D), 1.0, 6.0, ((0, 8),)),
        "cotangent": gaussian(keys[1], (IMAGES, SEQ, D), 1.0, 6.0, ((0, 8),)),
        "qkv_weight": gaussian(keys[2], (LAYERS, 3, D, D), D ** -0.5, 0.1875, ((2, 4), (3, 4))),
        "out_weight": gaussian(keys[3], (LAYERS, D, D), 4 ** -0.5, 3.0, ((1, 4), (2, 4))),
        "up_weight": gaussian(keys[4], (LAYERS, D, FF), D ** -0.5, 0.1875, ((1, 4), (2, 4))),
        "down_weight": gaussian(keys[5], (LAYERS, FF, D), FF ** -0.5, 0.09375, ((1, 4), (2, 4))),
        "query_bias": gaussian(keys[6], (LAYERS, HEADS, HD), 0.5, 3.0, ((1, 4), (2, 4))),
        "value_bias": gaussian(keys[7], (LAYERS, HEADS, HD), 0.03, 0.19921875, ((1, 4), (2, 4))),
        "up_bias": gaussian(keys[8], (LAYERS, HEADS, FF // HEADS), 0.5, 3.0, ((1, 4), (2, 4))),
        "norm_gain": jnp.clip(1.0 + 0.1 * jax.random.normal(keys[9], (LAYERS, 2, D), jnp.float32), 0.5, 1.5).astype(jnp.bfloat16),
        "norm_shift": gaussian(keys[10], (LAYERS, 4, D), 0.3, 2.0, ((2, 4),)),
    }


@jax.custom_vjp
def low(v):
    return lax.optimization_barrier(v.astype(jnp.bfloat16)).astype(jnp.float32)

@jax.custom_vjp
def low_back(v):
    return v

def low_keep(v):
    return (low(v), None)

def low_pass(kept, grad):
    return (grad,)

def back_keep(v):
    return (v, None)

def back_low(kept, grad):
    return (low(grad),)
low.defvjp(low_keep, low_pass)
low_back.defvjp(back_keep, back_low)
EPSILON = 1e-06

def product(left, right):
    return jnp.dot(left, right, precision=lax.Precision.HIGHEST)

def layer_norm(field, norm_gains, norm_shifts):
    average = lax.optimization_barrier(jnp.mean(field, -1, keepdims=True))
    centered = field - average
    variance = lax.optimization_barrier(jnp.mean(centered * centered, -1, keepdims=True))
    return centered * lax.rsqrt(variance + EPSILON) * norm_gains + norm_shifts

def block(residual, proj_qkv, proj_out, proj_up, proj_down, bias_query, bias_value, bias_up, norm_gains, norm_shifts):
    length = residual.shape[0]
    scale = 1.0 / math.sqrt(HD)
    normed = low(layer_norm(residual, norm_gains[0], norm_shifts[0]))
    queries = low(low_back(product(normed, proj_qkv[0]) + bias_query)).reshape(length, HEADS, HD)
    key_rows = low(low_back(product(normed, proj_qkv[1]))).reshape(length, HEADS, HD)
    value_rows = low(low_back(product(normed, proj_qkv[2]) + bias_value)).reshape(length, HEADS, HD)
    scores = low_back(jnp.einsum('qhd,khd->hqk', queries, key_rows, precision=lax.Precision.HIGHEST) * scale)
    attn_probs = low(jax.nn.softmax(scores, axis=-1))
    attn_mix = low(low_back(jnp.einsum('hqk,khd->qhd', attn_probs, value_rows, precision=lax.Precision.HIGHEST).reshape(length, D)))
    middle = residual + (low_back(product(attn_mix, proj_out)) + norm_shifts[2])
    normed_two = low(layer_norm(middle, norm_gains[1], norm_shifts[1]))
    up_values = low_back(product(normed_two, proj_up) + bias_up)
    hidden = low(jax.nn.gelu(up_values, approximate=False))
    return middle + (low_back(product(hidden, proj_down)) + norm_shifts[3])

def forward(image_rows, params):
    qkv_all, out_all, up_all, down_all, query_all, value_all, upbias_all, gain_all, shift_all = params
    residual = image_rows
    for layer_index in range(LAYERS):
        residual = block(residual, qkv_all[layer_index], out_all[layer_index], up_all[layer_index], down_all[layer_index], query_all[layer_index].reshape(D), value_all[layer_index].reshape(D), upbias_all[layer_index].reshape(FF), gain_all[layer_index], shift_all[layer_index])
    return residual

def reference(images, cotangent, qkv_weight, out_weight, up_weight, down_weight, query_bias, value_bias, up_bias, norm_gain, norm_shift):
    params = (qkv_weight.astype(jnp.float32), out_weight.astype(jnp.float32), up_weight.astype(jnp.float32), down_weight.astype(jnp.float32), query_bias.astype(jnp.float32), value_bias.astype(jnp.float32), up_bias.astype(jnp.float32), norm_gain.astype(jnp.float32), norm_shift.astype(jnp.float32))

    def per_image(totals, inputs):
        image_rows, cotangent_rows = inputs
        outputs, backward = jax.vjp(forward, image_rows.astype(jnp.float32), params)
        grad_rows, grad_params = backward(cotangent_rows.astype(jnp.float32))
        totals = jax.tree.map(jnp.add, totals, grad_params)
        return (totals, (outputs.astype(jnp.bfloat16), grad_rows.astype(jnp.bfloat16)))
    zeros_start = jax.tree.map(jnp.zeros_like, params)
    totals, (out_images, grad_images) = lax.scan(per_image, zeros_start, (images, cotangent))
    return (out_images, grad_images, totals[0], totals[1], totals[2], totals[3], totals[4], totals[5], totals[6], totals[7], totals[8])
```

```python
from functools import partial
import math

import jax
import jax.numpy as jnp
from jax import lax
from jax.sharding import PartitionSpec as P

HD = 64
SEQ = 577


EPSILON = 1e-06


def combine(partial_sum):
    return lax.psum(partial_sum.astype(jnp.bfloat16), "tensor").astype(jnp.float32)


def arrange(whole):
    (
        proj_qkv,
        proj_out,
        proj_up,
        proj_down,
        bias_query,
        bias_value,
        bias_up,
        norm_gains,
        norm_shifts,
    ) = whole
    return (
        proj_qkv,
        proj_out,
        proj_up,
        proj_down,
        bias_query.reshape(-1).astype(jnp.float32),
        bias_value.reshape(-1).astype(jnp.float32),
        bias_up.reshape(-1).astype(jnp.float32),
        norm_gains.astype(jnp.float32),
        norm_shifts.astype(jnp.float32),
    )


def norm_forward(field, norm_gain, norm_shift):
    average = jnp.mean(field, -1, keepdims=True)
    centered = field - average
    variance = jnp.mean(centered * centered, -1, keepdims=True)
    inverse = lax.rsqrt(variance + EPSILON)
    standard = centered * inverse
    return (standard * norm_gain + norm_shift, standard, inverse)


def norm_backward(grad_normed, norm_gain, standard, inverse):
    scaled = grad_normed * norm_gain
    return inverse * (
        scaled
        - jnp.mean(scaled, -1, keepdims=True)
        - standard * jnp.mean(scaled * standard, -1, keepdims=True)
    )


def attention_scores(queries, key_rows):
    return jnp.einsum("qhd,khd->hqk", queries, key_rows, preferred_element_type=jnp.float32) * (
        1.0 / math.sqrt(HD)
    )


def layer_forward(residual, weights):
    (
        proj_qkv,
        proj_out,
        proj_up,
        proj_down,
        bias_query,
        bias_value,
        bias_up,
        norm_gains,
        norm_shifts,
    ) = weights
    length = SEQ
    local_width = proj_qkv.shape[2]
    local_heads = local_width // HD
    normed, standard_one, inverse_one = norm_forward(residual, norm_gains[0], norm_shifts[0])
    normed_low = normed.astype(jnp.bfloat16)
    queries = (
        (jnp.dot(normed_low, proj_qkv[0], preferred_element_type=jnp.float32) + bias_query)
        .astype(jnp.bfloat16)
        .reshape(length, local_heads, HD)
    )
    key_rows = (
        jnp.dot(normed_low, proj_qkv[1], preferred_element_type=jnp.float32)
        .astype(jnp.bfloat16)
        .reshape(length, local_heads, HD)
    )
    value_rows = (
        (jnp.dot(normed_low, proj_qkv[2], preferred_element_type=jnp.float32) + bias_value)
        .astype(jnp.bfloat16)
        .reshape(length, local_heads, HD)
    )
    scores = attention_scores(queries, key_rows)
    highest = jnp.max(scores, -1, keepdims=True)
    log_total = highest + jnp.log(jnp.sum(jnp.exp(scores - highest), -1, keepdims=True))
    attn_probs = jnp.exp(scores - log_total).astype(jnp.bfloat16)
    attn_mix = (
        jnp.einsum("hqk,khd->qhd", attn_probs, value_rows, preferred_element_type=jnp.float32)
        .reshape(length, local_width)
        .astype(jnp.bfloat16)
    )
    attn_out = combine(jnp.dot(attn_mix, proj_out, preferred_element_type=jnp.float32))
    middle = residual + (attn_out + norm_shifts[2])
    normed_two, standard_two, inverse_two = norm_forward(middle, norm_gains[1], norm_shifts[1])
    normed_two_low = normed_two.astype(jnp.bfloat16)
    up_values = jnp.dot(normed_two_low, proj_up, preferred_element_type=jnp.float32) + bias_up
    hidden = jax.nn.gelu(up_values, approximate=False).astype(jnp.bfloat16)
    mlp_out = combine(jnp.dot(hidden, proj_down, preferred_element_type=jnp.float32))
    result = middle + (mlp_out + norm_shifts[3])
    stored = (
        standard_one,
        inverse_one,
        normed_low,
        queries,
        key_rows,
        value_rows,
        log_total,
        attn_mix,
        standard_two,
        inverse_two,
        normed_two_low,
        up_values,
        hidden,
    )
    return (result, stored)


def layer_backward(grad_top, weights, stored):
    (
        proj_qkv,
        proj_out,
        proj_up,
        proj_down,
        bias_query,
        bias_value,
        bias_up,
        norm_gains,
        norm_shifts,
    ) = weights
    (
        standard_one,
        inverse_one,
        normed_low,
        queries,
        key_rows,
        value_rows,
        log_total,
        attn_mix,
        standard_two,
        inverse_two,
        normed_two_low,
        up_values,
        hidden,
    ) = stored
    length = SEQ
    local_width = proj_qkv.shape[2]
    local_heads = local_width // HD
    scale = 1.0 / math.sqrt(HD)
    grad_down_bias = jnp.sum(grad_top, 0)
    grad_low = grad_top.astype(jnp.bfloat16)
    grad_down = jnp.einsum("sf,sd->fd", hidden, grad_low, preferred_element_type=jnp.float32)
    grad_hidden = jnp.einsum("sd,fd->sf", grad_low, proj_down, preferred_element_type=jnp.float32)
    gelu_back = jax.vjp(partial(jax.nn.gelu, approximate=False), up_values)[1]
    grad_up_values = gelu_back(grad_hidden)[0].astype(jnp.bfloat16)
    grad_bias_up = jnp.sum(grad_up_values, 0, dtype=jnp.float32)
    grad_up = jnp.einsum(
        "sd,sf->df", normed_two_low, grad_up_values, preferred_element_type=jnp.float32
    )
    grad_normed_two = combine(
        jnp.einsum("sf,df->sd", grad_up_values, proj_up, preferred_element_type=jnp.float32)
    )
    grad_gain_two = jnp.sum(grad_normed_two * standard_two, 0)
    grad_shift_two = jnp.sum(grad_normed_two, 0)
    grad_middle = grad_top + norm_backward(
        grad_normed_two, norm_gains[1], standard_two, inverse_two
    )
    grad_out_bias = jnp.sum(grad_middle, 0)
    grad_middle_low = grad_middle.astype(jnp.bfloat16)
    grad_proj_out = jnp.einsum(
        "sw,sd->wd", attn_mix, grad_middle_low, preferred_element_type=jnp.float32
    )
    grad_mix = (
        jnp.einsum("sd,wd->sw", grad_middle_low, proj_out, preferred_element_type=jnp.float32)
        .astype(jnp.bfloat16)
        .reshape(length, local_heads, HD)
    )
    attn_probs = jnp.exp(attention_scores(queries, key_rows) - log_total)
    grad_values = (
        jnp.einsum(
            "hqk,qhd->khd",
            attn_probs.astype(jnp.bfloat16),
            grad_mix,
            preferred_element_type=jnp.float32,
        )
        .astype(jnp.bfloat16)
        .reshape(length, local_width)
    )
    grad_probs = jnp.einsum(
        "qhd,khd->hqk", grad_mix, value_rows, preferred_element_type=jnp.float32
    )
    grad_scores = (
        attn_probs * (grad_probs - jnp.sum(grad_probs * attn_probs, -1, keepdims=True))
    ).astype(jnp.bfloat16)
    grad_queries = (
        (
            jnp.einsum("hqk,khd->qhd", grad_scores, key_rows, preferred_element_type=jnp.float32)
            * scale
        )
        .astype(jnp.bfloat16)
        .reshape(length, local_width)
    )
    grad_keys = (
        (
            jnp.einsum("hqk,qhd->khd", grad_scores, queries, preferred_element_type=jnp.float32)
            * scale
        )
        .astype(jnp.bfloat16)
        .reshape(length, local_width)
    )
    grad_rows = jnp.stack([grad_queries, grad_keys, grad_values])
    grad_qkv = jnp.einsum("sd,tsw->tdw", normed_low, grad_rows, preferred_element_type=jnp.float32)
    grad_normed = combine(
        jnp.einsum("tsw,tdw->sd", grad_rows, proj_qkv, preferred_element_type=jnp.float32)
    )
    grad_gain_one = jnp.sum(grad_normed * standard_one, 0)
    grad_shift_one = jnp.sum(grad_normed, 0)
    grad_input = grad_middle + norm_backward(grad_normed, norm_gains[0], standard_one, inverse_one)
    gradients = (
        grad_qkv,
        grad_proj_out,
        grad_up,
        grad_down,
        jnp.sum(grad_queries, 0, dtype=jnp.float32).reshape(local_heads, HD),
        jnp.sum(grad_values, 0, dtype=jnp.float32).reshape(local_heads, HD),
        grad_bias_up.reshape(local_heads, -1),
        jnp.stack([grad_gain_one, grad_gain_two]),
        jnp.stack([grad_shift_one, grad_shift_two, grad_out_bias, grad_down_bias]),
    )
    return (grad_input, gradients)


def on_device(
    images,
    cotangent,
    qkv_weight,
    out_weight,
    up_weight,
    down_weight,
    query_bias,
    value_bias,
    up_bias,
    norm_gain,
    norm_shift,
):
    layers = qkv_weight.shape[0]
    owners = lax.axis_size("fsdp")
    index = lax.axis_index("fsdp")
    smalls = (query_bias, value_bias, up_bias, norm_gain, norm_shift)
    packed = jnp.concatenate([member.reshape(-1) for member in smalls])
    gathered = lax.all_gather(packed, "fsdp", axis=0)
    whole_small = []
    offset = 0
    for member in smalls:
        part = gathered[:, offset : offset + member.size].reshape((owners,) + member.shape)
        offset += member.size
        part = jnp.moveaxis(part, 0, 2)
        whole_small.append(part.reshape(member.shape[:2] + (owners * member.shape[2],)))
    weights = []
    for layer_index in range(layers):
        weights.append(
            arrange(
                (
                    lax.all_gather(qkv_weight[layer_index], "fsdp", axis=1, tiled=True),
                    lax.all_gather(out_weight[layer_index], "fsdp", axis=1, tiled=True),
                    lax.all_gather(up_weight[layer_index], "fsdp", axis=0, tiled=True),
                    lax.all_gather(down_weight[layer_index], "fsdp", axis=1, tiled=True),
                )
                + tuple(member[layer_index] for member in whole_small)
            )
        )
    count = images.shape[0]
    residuals = [images[i].astype(jnp.float32) for i in range(count)]
    stored = []
    for layer_index in range(layers):
        kept_all = []
        for i in range(count):
            residuals[i], kept = layer_forward(residuals[i], weights[layer_index])
            kept_all.append(kept)
        stored.append(kept_all)
    out_images = jnp.stack([r.astype(jnp.bfloat16) for r in residuals])
    gradients = [cotangent[i].astype(jnp.float32) for i in range(count)]
    per_layer = [None] * layers
    for layer_index in reversed(range(layers)):
        total = None
        for i in range(count):
            gradients[i], grads = layer_backward(
                gradients[i], weights[layer_index], stored[layer_index][i]
            )
            total = grads if total is None else tuple(a + b for a, b in zip(total, grads))
        flat = []
        for member, axis in zip(total, (1, 1, 0, 1, 1, 1, 1, 1, 1)):
            shape = member.shape
            split = member.reshape(
                shape[:axis] + (owners, shape[axis] // owners) + shape[axis + 1 :]
            )
            flat.append(jnp.moveaxis(split, axis, 0).astype(jnp.bfloat16).reshape(owners, -1))
        joined = jnp.concatenate(flat, 1)
        owned = lax.psum_scatter(joined, "fsdp", scatter_dimension=0, tiled=True)
        owned = lax.psum(owned, "dp").astype(jnp.float32).reshape(-1)
        pieces = []
        offset = 0
        for member, axis in zip(total, (1, 1, 0, 1, 1, 1, 1, 1, 1)):
            shape = list(member.shape)
            shape[axis] //= owners
            size = math.prod(shape)
            pieces.append(owned[offset : offset + size].reshape(shape))
            offset += size
        per_layer[layer_index] = pieces
    grad_images = jnp.stack([g.astype(jnp.bfloat16) for g in gradients])
    stacked = tuple(
        jnp.stack([per_layer[layer_index][m] for layer_index in range(layers)]) for m in range(9)
    )
    return (out_images, grad_images) + stacked


def solution(mesh):
    in_specs = (
        P(("dp", "fsdp"), None, None),
        P(("dp", "fsdp"), None, None),
        P(None, None, "fsdp", "tensor"),
        P(None, "tensor", "fsdp"),
        P(None, "fsdp", "tensor"),
        P(None, "tensor", "fsdp"),
        P(None, "tensor", "fsdp"),
        P(None, "tensor", "fsdp"),
        P(None, "tensor", "fsdp"),
        P(None, None, "fsdp"),
        P(None, None, "fsdp"),
    )
    out_specs = (
        P(("dp", "fsdp"), None, None),
        P(("dp", "fsdp"), None, None),
        P(None, None, "fsdp", "tensor"),
        P(None, "tensor", "fsdp"),
        P(None, "fsdp", "tensor"),
        P(None, "tensor", "fsdp"),
        P(None, "tensor", "fsdp"),
        P(None, "tensor", "fsdp"),
        P(None, "tensor", "fsdp"),
        P(None, None, "fsdp"),
        P(None, None, "fsdp"),
    )
    return jax.shard_map(
        on_device, mesh=mesh, in_specs=in_specs, out_specs=out_specs, check_vma=False
    )
```

```python
import math

import jax
import jax.numpy as jnp
from jax import lax
from jax.experimental import pallas as pl
from jax.experimental.pallas import tpu as pltpu
from jax.sharding import PartitionSpec as P

BF = jnp.bfloat16
F32 = jnp.float32
MESH = pl.DeviceIdType.MESH
ANY = pl.BlockSpec(memory_space=pl.ANY)
EPSILON = 1e-06
HD = 64
SEQ = 577
PAD = 608
HALF = PAD // 2
KEYS = 640
NEG = -1e30
D = 1024
WIDE = 512


def dot(a, b, ca=1, cb=0):
    return lax.dot_general(a, b, (((ca,), (cb,)), ((), ())), preferred_element_type=F32)


def rows16(i, size=16):
    return pl.ds(pl.multiple_of(i * size, size), size)


def remote(src, dst, ssem, rsem, where):
    return pltpu.make_async_remote_copy(
        src_ref=src,
        dst_ref=dst,
        send_sem=ssem,
        recv_sem=rsem,
        device_id=where,
        device_id_type=MESH,
    )


class Here:
    def __init__(self):
        self.dp = lax.axis_index("dp")
        self.f = lax.axis_index("fsdp")
        t = lax.axis_index("tensor")
        self.core = lax.rem(t, 2)
        self.y = lax.div(t, 2)
        self.core_mate = {"tensor": self.y * 2 + (1 - self.core)}
        self.y_mate = {"tensor": (1 - self.y) * 2 + self.core}
        self.x_mate = {"dp": 1 - self.dp}
        self.own = pl.ds(pl.multiple_of(self.core * HALF, 16), HALF)
        self.mate = pl.ds(pl.multiple_of((1 - self.core) * HALF, 16), HALF)

    def peer(self, n, k):
        return lax.rem(self.f + k, n)

    def greet(self, n):
        barrier = pltpu.get_barrier_semaphore()
        for where in (self.core_mate, self.y_mate, self.x_mate):
            pl.semaphore_signal(barrier, inc=1, device_id=where, device_id_type=MESH)

        def each(k, carry):
            pl.semaphore_signal(
                barrier, inc=1, device_id={"fsdp": self.peer(n, k)}, device_id_type=MESH
            )
            return carry

        lax.fori_loop(1, n, each, 0)
        pl.semaphore_wait(barrier, n + 2)


def standardize(v):
    centered = v - jnp.sum(v, -1, keepdims=True) * (1.0 / D)
    inverse = lax.rsqrt(jnp.sum(centered * centered, -1, keepdims=True) * (1.0 / D) + EPSILON)
    return centered * inverse, inverse


def take_rows(here, whole, half):
    full = (SEQ - HALF) // 16

    def copy(k, carry):
        there = pl.ds(pl.multiple_of(here.core * HALF + k * 16, 16), 16)
        half[rows16(k), :] = whole[there, :].astype(F32)
        return carry

    lax.fori_loop(0, full, copy, 0)

    @pl.when(here.core == 0)
    def _():
        half[full * 16 : HALF, :] = whole[full * 16 : HALF, :].astype(F32)

    @pl.when(here.core == 1)
    def _():
        half[full * 16 : HALF, :] = jnp.zeros((HALF - full * 16, D), F32)
        half[full * 16 : full * 16 + 1, :] = whole[SEQ - 1 : SEQ, :].astype(F32)


def drop_rows(padded, whole):
    def copy(k, carry):
        whole[rows16(k), :] = padded[rows16(k), :]
        return carry

    lax.fori_loop(0, SEQ // 16, copy, 0)
    whole[SEQ - 1 : SEQ, :] = padded[SEQ - 1 : SEQ, :]


def forward_kernel(
    n,
    img,
    wsh,
    pk,
    w_all,
    n_all,
    qkv_all,
    o_all,
    g_all,
    gp_all,
    r_all,
    prm_all,
    out_all,
    imgv,
    wa,
    wu,
    wd,
    nb,
    rb,
    ysend,
    yrecv,
    psend,
    pown,
    precv,
    qkvb,
    ob,
    gb,
    gpb,
    ub,
    sb,
    pb,
    lb,
    pkr,
    prm,
    zs,
    zr,
    xs,
    xr,
    ks,
    kr,
    ys,
    yr,
    ps,
    pr,
    cs,
    cr,
    lw,
    lv,
    li,
    sn,
    sr,
    sq,
    sg,
    so,
):
    here = Here()
    f, dp = here.f, here.dp
    piece_rows = D // n
    half_rows = piece_rows // 2
    units = 2 * wsh.shape[0]
    here.greet(n)

    pkr[f] = pk[...]

    def small_copy(k):
        return remote(
            pk, pkr.at[f], ks.at[k], kr.at[k], {"fsdp": here.peer(n, k)}
        )

    def small_start(k, carry):
        small_copy(k).start()
        return carry

    def small_wait(k, carry):
        source = lax.rem(f + n - k, n)
        remote(pk, pkr.at[source], ks.at[k], kr.at[k], {"fsdp": source}).wait_recv()
        return carry

    def small_sent(k, carry):
        small_copy(k).wait_send()
        return carry

    lax.fori_loop(1, n, small_start, 0)

    def place(u, shard):
        return w_all.at[
            u // 2,
            pl.ds(pl.multiple_of(shard * piece_rows + dp * half_rows, half_rows), half_rows),
            pl.ds((u % 2) * WIDE, WIDE),
        ]

    def mine(u):
        return wsh.at[
            u // 2,
            pl.ds(pl.multiple_of(dp * half_rows, half_rows), half_rows),
            pl.ds((u % 2) * WIDE, WIDE),
        ]

    def other_half(u, shard):
        return w_all.at[
            u // 2,
            pl.ds(
                pl.multiple_of(shard * piece_rows + (1 - dp) * half_rows, half_rows), half_rows
            ),
            pl.ds((u % 2) * WIDE, WIDE),
        ]

    def ahead(way):
        return {"fsdp": jnp.clip(f + (1 if way == 0 else -1), 0, n - 1)}

    def arrives(way, j):
        return (f >= j) if way == 0 else (f + j <= n - 1)

    def leaves(way, j):
        more = (f < n - 1) if way == 0 else (f > 0)
        return jnp.logical_and(more, arrives(way, j))

    def shard_of(way, j):
        return jnp.clip(f - j if way == 0 else f + j, 0, n - 1)

    def z_copy(u, way, j, first):
        src = mine(u) if first else place(u, shard_of(way, j))
        return remote(
            src,
            place(u, shard_of(way, j)),
            zs.at[way, u, j],
            zr.at[way, u, j + 1],
            ahead(way),
        )

    def x_copy(u, way, j):
        at = place(u, shard_of(way, j))
        return remote(at, at, xs.at[way, u, j], xr.at[way, u, j], here.x_mate)

    def hop(u, j, first=False, last=False):
        for way in (0, 1):
            if not first:

                @pl.when(arrives(way, j))
                def _():
                    at = place(u, shard_of(way, j))
                    remote(at, at, zs.at[way, u, j], zr.at[way, u, j], ahead(way)).wait_recv()

            if not last:

                @pl.when(leaves(way, j))
                def _():
                    z_copy(u, way, j, first).start()

            if not first:

                @pl.when(arrives(way, j))
                def _():
                    x_copy(u, way, j).start()

    def turn(r):
        if n > 4:
            u = r - 3
            if 0 <= u < units:
                hop(u, 0, first=True)

                def each(j, carry):
                    hop(u, j)
                    return carry

                lax.fori_loop(1, n - 1, each, 0)
                hop(u, n - 1, last=True)
            return
        for j in reversed(range(n)):
            if 0 <= r - j < units:
                hop(r - j, j, first=j == 0, last=j == n - 1)

    def take(u, buffer, slot):
        def each(j, carry):
            for way in (0, 1):

                @pl.when(arrives(way, j))
                def _():
                    at = other_half(u, shard_of(way, j))
                    remote(at, at, xs.at[way, u, j], xr.at[way, u, j], here.x_mate).wait_recv()

            return carry

        lax.fori_loop(1, n, each, 0)
        if u % 2 == 0:
            own_copy(u // 2).wait()
        cols = pl.ds((u % 2) * WIDE, WIDE)
        copy = pltpu.make_async_copy(w_all.at[u // 2, :, cols], buffer.at[:, cols], lv.at[u])
        copy.start()
        copy.wait()

    def all_sent():
        for u in range(units):

            def each(j, carry):
                for way in (0, 1):

                    @pl.when(leaves(way, j))
                    def _():
                        z_copy(u, way, j, False).wait_send()

                    @pl.when(jnp.logical_and(j > 0, arrives(way, j)))
                    def _():
                        x_copy(u, way, j).wait_send()

                return carry

            lax.fori_loop(0, n, each, 0)

    def own_copy(p):
        at = pl.ds(pl.multiple_of(f * piece_rows, piece_rows), piece_rows)
        return pltpu.make_async_copy(wsh.at[p], w_all.at[p, at], lw.at[p])

    turn(0)
    for p in range(wsh.shape[0]):
        own_copy(p).start()

    loads = []
    for i in (0, 1):
        qkvb[i, PAD:KEYS, :] = jnp.zeros((KEYS - PAD, 768), BF)
        loads.append(pltpu.make_async_copy(img.at[i], imgv.at[i], li.at[i]))
        loads[i].start()
    lax.fori_loop(1, n, small_wait, 0)
    total = pkr[0].astype(F32)
    for k in range(1, n):
        total = total + pkr[k].astype(F32)
    prm[...] = total
    turn(1)

    saves = {}

    def save(name, src, dst, sem):
        copy = pltpu.make_async_copy(src, dst, sem)
        copy.start()
        saves[name] = copy

    def settle(name):
        if name in saves:
            saves.pop(name).wait()

    pending = {}

    def share(t):
        copy = remote(
            nb.at[t % 4, here.own], nb.at[t % 4, here.own], cs.at[t], cr.at[t], here.core_mate
        )
        copy.start()
        pending[t] = copy

    def shared(t):
        pending.pop(t).wait()
        if t < 8:
            save(("n", t), nb.at[t % 4], n_all.at[t], sn.at[t])

    for i in (0, 1):
        loads[i].wait()
        take_rows(here, imgv.at[i], rb.at[i])

        standard, _ = standardize(rb[i])
        nb[i, here.own, :] = (standard * prm[0:1, :] + prm[1:2, :]).astype(BF)
        share(i)
        save(("r", i), rb.at[i], r_all.at[i], sr.at[i])

    def exchange(t, left, right_block):
        slot = t % 2
        for c in (0, 1):
            cols = slice(c * 512, c * 512 + 512)
            psend[slot, :, cols] = dot(left(here.mate), right_block(c), 1, 1).astype(BF)
        copy = remote(psend.at[slot], precv.at[t], ps.at[t], pr.at[t], here.core_mate)
        copy.start()
        for c in (0, 1):
            cols = slice(c * 512, c * 512 + 512)
            pown[:, cols] = dot(left(here.own), right_block(c), 1, 1)
        copy.wait()

        ysend[slot] = (pown[...] + precv[t].astype(F32)).astype(BF)
        y_copy = remote(ysend.at[slot], yrecv.at[t], ys.at[t], yr.at[t], here.y_mate)
        y_copy.start()
        pending[("y", t)] = y_copy

    def finish(t):
        i, layer, mlp = t % 2, t // 4, (t // 2) % 2
        slot = t % 2
        pending.pop(("y", t)).wait()
        settle(("r", t))
        bias = prm[layer * 8 + (5 if mlp else 2)][None]
        base = (layer + 1) * 8 if mlp else layer * 8 + 3
        last = t >= 6
        if not last:
            gain, shift = prm[base][None], prm[base + 1][None]

        v = rb[i] + ((ysend[slot].astype(F32) + yrecv[t].astype(F32)) + bias)
        if last:
            nb[(t + 2) % 4, here.own, :] = v.astype(BF)
        else:
            rb[i] = v
            standard, _ = standardize(v)
            nb[(t + 2) % 4, here.own, :] = (standard * gain + shift).astype(BF)
        share(t + 2)
        if not last:
            save(("r", t + 2), rb.at[i], r_all.at[t + 2], sr.at[t + 2])

    lane = lax.broadcasted_iota(jnp.int32, (PAD, KEYS), 1)

    def attention(t):
        i, layer = t % 2, t // 4
        settle(("n", t - 2))
        settle(("qkv", i))
        settle(("o", i))
        shared(t)
        for c0, c1 in ((0, 512), (512, 768)):
            acc = dot(nb[t % 4], wa[:, c0:c1])
            qkvb[i, 0:PAD, c0:c1] = (acc + prm[layer * 8 + 7, c0:c1][None]).astype(BF)
        save(("qkv", i), qkvb.at[i, pl.ds(0, PAD)], qkv_all.at[layer * 2 + i], sq.at[layer * 2 + i])
        for h in range(4):
            q = qkvb[i, 0:PAD, h * HD : h * HD + HD]
            k_rows = qkvb[i, :, 256 + h * HD : 256 + h * HD + HD]
            v_rows = qkvb[i, :, 512 + h * HD : 512 + h * HD + HD]
            sb[...] = dot(q, k_rows, 1, 1)

            s = jnp.where(lane < SEQ, sb[...], NEG)
            e = jnp.exp((s - jnp.max(s, -1, keepdims=True)) * (1.0 / math.sqrt(HD)))
            pb[...] = e.astype(BF)
            lb[...] = jnp.broadcast_to(1.0 / jnp.sum(e, -1, keepdims=True), (PAD, 128))
            ob[i, :, h * HD : h * HD + HD] = (dot(pb[...], v_rows) * lb[:, 0:HD]).astype(BF)
        save(("o", i), ob.at[i], o_all.at[layer * 2 + i], so.at[layer * 2 + i])
        exchange(
            t,
            lambda at: ob[i, at, :],
            lambda c: wa[c * 512 : c * 512 + 512, 768:1024],
        )

    def hidden(t):
        i, layer = t % 2, t // 4
        settle(("n", t - 2))
        settle(("g", i))
        settle(("gp", i))
        shared(t)
        for c in (0, 1):
            cols = slice(c * 512, c * 512 + 512)
            ub[...] = dot(nb[t % 4], wu[:, cols])
            bias = prm[layer * 8 + 6, cols][None]

            u = ub[...] + bias
            phi = 0.5 * (1.0 + lax.erf(u * math.sqrt(0.5)))
            density = jnp.exp(u * u * -0.5) * (1.0 / math.sqrt(2.0 * math.pi))
            gb[i, :, cols] = (u * phi).astype(BF)
            gpb[i, :, cols] = (phi + u * density).astype(BF)
        save(("g", i), gb.at[i], g_all.at[layer * 2 + i], sg.at[layer * 2 + i])
        save(("gp", i), gpb.at[i], gp_all.at[layer * 2 + i], sg.at[4 + layer * 2 + i])

    def project(t):
        i = t % 2
        exchange(t, lambda at: gb[i, at, :], lambda c: wd[c * 512 : c * 512 + 512, :])

    def turns(*which):
        for r in which:
            turn(r)

    turns(2, 3)
    take(0, wa, 0)
    turn(4)
    take(1, wa, 0)
    attention(0)
    turn(5)
    attention(1)
    finish(0)
    turn(6)
    take(2, wu, 1)
    take(3, wu, 1)
    hidden(2)
    finish(1)
    hidden(3)
    turns(7, 8)
    take(4, wd, 2)
    take(5, wd, 2)
    project(2)
    turn(9)
    project(3)
    finish(2)
    turn(10)
    take(6, wa, 0)
    take(7, wa, 0)
    attention(4)
    turn(11)
    finish(3)
    attention(5)
    finish(4)
    turn(12)
    take(8, wu, 1)
    take(9, wu, 1)
    hidden(6)
    finish(5)
    hidden(7)
    turns(13, 14)
    take(10, wd, 2)
    take(11, wd, 2)
    project(6)
    project(7)
    for t in (6, 7):
        settle(("n", t))
    for t in (6, 7):
        finish(t)
    params = pltpu.make_async_copy(prm, prm_all, li.at[0])
    params.start()
    for t in (8, 9):
        shared(t)
        drop_rows(nb.at[t % 4], imgv.at[t - 8])
        save(("out", t), imgv.at[t - 8], out_all.at[t - 8], li.at[t - 7])
    for name in list(saves):
        settle(name)
    params.wait()
    lax.fori_loop(1, n, small_sent, 0)
    all_sent()


def forward(n, images, wsh, pk):
    pieces = wsh.shape[0]
    units = 2 * pieces
    sds = jax.ShapeDtypeStruct
    dma = pltpu.SemaphoreType.DMA
    vm = pltpu.VMEM
    return pl.pallas_call(
        lambda *refs: forward_kernel(n, *refs),
        out_shape=(
            sds((pieces, D, D), BF),
            sds((8, PAD, D), BF),
            sds((4, PAD, 768), BF),
            sds((4, PAD, 256), BF),
            sds((4, PAD, D), BF),
            sds((4, PAD, D), BF),
            sds((8, HALF, D), F32),
            sds((16, D), F32),
            sds((2, SEQ, D), BF),
        ),
        in_specs=[ANY, ANY, pl.BlockSpec(memory_space=pltpu.VMEM)],
        out_specs=[ANY] * 9,
        scratch_shapes=[
            vm((2, SEQ, D), BF),
            vm((D, D), BF),
            vm((D, D), BF),
            vm((D, D), BF),
            vm((4, PAD, D), BF),
            vm((2, HALF, D), F32),
            vm((2, HALF, D), BF),
            vm((8, HALF, D), BF),
            vm((2, HALF, D), BF),
            vm((HALF, D), F32),
            vm((8, HALF, D), BF),
            vm((2, KEYS, 768), BF),
            vm((2, PAD, 256), BF),
            vm((2, PAD, D), BF),
            vm((2, PAD, D), BF),
            vm((PAD, 512), F32),
            vm((PAD, KEYS), F32),
            vm((PAD, KEYS), BF),
            vm((PAD, 128), F32),
            vm((n, 16, D), BF),
            vm((16, D), F32),
            dma((2, units, n)),
            dma((2, units, n + 1)),
            dma((2, units, n)),
            dma((2, units, n)),
            dma((n,)),
            dma((n,)),
            dma((8,)),
            dma((8,)),
            dma((8,)),
            dma((8,)),
            dma((10,)),
            dma((10,)),
            dma((pieces,)),
            dma((units,)),
            dma((4,)),
            dma((8,)),
            dma((8,)),
            dma((4,)),
            dma((8,)),
            dma((4,)),
        ],
        compiler_params=pltpu.CompilerParams(
            collective_id=0, has_side_effects=True, vmem_limit_bytes=60 << 20
        ),
        name="forward",
    )(images, wsh, pk)


def placed(piece, n, f):
    shape = piece.shape[:-1] + (n, piece.shape[-1])
    at = lax.broadcasted_iota(jnp.int32, shape, len(shape) - 2)
    full = jnp.where(at == f, piece[..., None, :], jnp.zeros((), piece.dtype))
    return full.reshape(shape[:-2] + (n * piece.shape[-1],))


def pack_small(n, query_bias, value_bias, up_bias, norm_gain, norm_shift):
    f = lax.axis_index("fsdp")
    layers = query_bias.shape[0]
    gain = placed(norm_gain, n, f)
    shift = placed(norm_shift, n, f)
    query = placed(query_bias, n, f).reshape(layers, -1)
    value = placed(value_bias, n, f).reshape(layers, -1)
    up = placed(up_bias, n, f).reshape(layers, -1)
    zero = jnp.zeros_like(query)
    rows = [
        gain[:, 0],
        shift[:, 0],
        shift[:, 2],
        gain[:, 1],
        shift[:, 1],
        shift[:, 3],
        up,
        jnp.concatenate([query, zero, value, zero], -1),
    ]
    return jnp.stack(rows, 1).reshape(layers * 8, D)


def pack_weights(qkv_weight, out_weight, up_weight, down_weight):
    pieces = []
    for layer in range(qkv_weight.shape[0]):
        w = qkv_weight[layer]
        pieces.append(jnp.concatenate([w[0], w[1], w[2], out_weight[layer].T], 1))
        pieces.append(up_weight[layer])
        pieces.append(down_weight[layer].T)
    return jnp.stack(pieces)


def backward_kernel(
    n,
    cot,
    w_all,
    n_all,
    qkv_all,
    o_all,
    g_all,
    gp_all,
    r_all,
    prm,
    gi_all,
    gw_all,
    small_all,
    xrecv,
    zrecv,
    cotv,
    wa,
    wu,
    wd,
    eb,
    er,
    rl,
    gb,
    gpb,
    nb,
    qkvb,
    ob,
    eub,
    ysend,
    yrecv,
    psend,
    pown,
    precv,
    sb,
    ep,
    pb,
    esb,
    eob,
    gst,
    xst,
    fsend,
    frecv,
    outv,
    sm,
    smc,
    smx,
    smz,
    ys,
    yr,
    ps,
    pr,
    cs,
    cr,
    ls,
    gxs,
    gxr,
    gzs,
    gzr,
    gfs,
    gfr,
    ks,
    kr,
):
    here = Here()
    f, dp = here.f, here.dp
    piece_rows = D // n
    half_rows = piece_rows // 2
    scale = 1.0 / math.sqrt(HD)
    here.greet(n)

    flying = {}
    count = [0]

    def load(name, src, dst):
        copy = pltpu.make_async_copy(src, dst, ls.at[count[0]])
        count[0] += 1
        copy.start()
        flying[name] = copy

    def need(*names):
        for name in names:
            if name in flying:
                flying.pop(name).wait()

    def load_hidden(layer):
        for i in (0, 1):
            load(("gp", i), gp_all.at[layer * 2 + i], gpb.at[i])
        for i in (0, 1):
            load(("g", i), g_all.at[layer * 2 + i], gb.at[i])
            load(("n2", i), n_all.at[layer * 4 + 2 + i], nb.at[2 + i])

    def load_attention(layer):
        for i in (0, 1):
            load(("qkv", i), qkv_all.at[layer * 2 + i], qkvb.at[i, pl.ds(0, PAD)])
            load(("o", i), o_all.at[layer * 2 + i], ob.at[i])
            load(("n1", i), n_all.at[layer * 4 + i], nb.at[i])

    load("wd", w_all.at[5], wd)
    for i in (0, 1):
        load(("cot", i), cot.at[i], cotv.at[i])
    load("wu", w_all.at[4], wu)
    load_hidden(1)
    for i in (0, 1):
        load(("r", i), r_all.at[4 + 2 + i], rl.at[i])
    load("wa", w_all.at[3], wa)
    load_attention(1)

    sm[...] = jnp.zeros_like(sm)
    for i in (0, 1):
        qkvb[i, PAD:KEYS, :] = jnp.zeros((KEYS - PAD, 768), BF)

    def tally(row, value, cols=slice(0, D)):
        sm[row : row + 1, cols] = sm[row : row + 1, cols] + jnp.sum(value, 0, keepdims=True)

    for i in (0, 1):
        need(("cot", i))
        take_rows(here, cotv.at[i], er.at[i])
        eb[i, 576:PAD, :] = jnp.zeros((PAD - 576, D), BF)
        eb[i, 0:SEQ, :] = cotv[i]
        tally(8 + 5, er[i])

    pending = {}

    def share(t):
        copy = remote(
            eb.at[t % 4, here.own], eb.at[t % 4, here.own], cs.at[t], cr.at[t], here.core_mate
        )
        copy.start()
        pending[t] = copy

    def shared(t):
        if t in pending:
            pending.pop(t).wait()

    def exchange(t, left, right_block):
        slot = t % 2
        for c in (0, 1):
            cols = slice(c * 512, c * 512 + 512)
            psend[slot, :, cols] = dot(left(here.mate), right_block(c), 1, 1).astype(BF)
        copy = remote(psend.at[slot], precv.at[slot], ps.at[t], pr.at[t], here.core_mate)
        copy.start()
        for c in (0, 1):
            cols = slice(c * 512, c * 512 + 512)
            pown[:, cols] = dot(left(here.own), right_block(c), 1, 1)
        copy.wait()
        ysend[slot] = (pown[...] + precv[slot].astype(F32)).astype(BF)
        y_copy = remote(ysend.at[slot], yrecv.at[t % 4], ys.at[t], yr.at[t], here.y_mate)
        y_copy.start()
        pending[("y", t)] = y_copy

    def finish(t):
        i, layer, mlp = t % 2, 1 - t // 4, 1 - (t // 2) % 2
        slot = t % 2
        pending.pop(("y", t)).wait()
        need(("r", i))
        e = ysend[slot].astype(F32) + yrecv[t % 4].astype(F32)
        standard, inverse = standardize(rl[i])
        base = layer * 8 + (3 if mlp else 0)
        tally(base, e * standard)
        tally(base + 1, e)
        scaled = e * prm[base : base + 1, :]
        grad = inverse * (
            scaled
            - jnp.sum(scaled, -1, keepdims=True) * (1.0 / D)
            - standard * (jnp.sum(scaled * standard, -1, keepdims=True) * (1.0 / D))
        )
        total = er[i] + grad
        er[i] = total
        if mlp:
            tally(layer * 8 + 2, total)
        elif layer > 0:
            tally((layer - 1) * 8 + 5, total)
        eb[(t + 2) % 4, here.own, :] = total.astype(BF)
        share(t + 2)
        if t + 2 < 8:
            into = t + 2
            at = (1 - into // 4) * 4 + (2 if (into // 2) % 2 == 0 else 0) + i
            load(("r", i), r_all.at[at], rl.at[i])

    def hidden(t):
        i, layer = t % 2, 1 - t // 4
        shared(t)
        need("wd", ("gp", i))
        for c in (0, 1):
            cols = slice(c * 512, c * 512 + 512)
            eu = (dot(eb[t % 4], wd[:, cols]) * gpb[i, :, cols].astype(F32)).astype(BF)
            eub[i, :, cols] = eu
            tally(layer * 8 + 6, eu.astype(F32), cols)
        need("wu")
        exchange(t, lambda at: eub[i, at, :], lambda c: wu[c * 512 : c * 512 + 512, :])

    lane = lax.broadcasted_iota(jnp.int32, (PAD, KEYS), 1)

    def attention(t):
        i, layer = t % 2, 1 - t // 4
        shared(t)
        need("wa", ("qkv", i))
        eob[...] = dot(eb[t % 4], wa[:, 768:1024]).astype(BF)
        for h in range(4):
            at = [slice(256 * m + h * HD, 256 * m + h * HD + HD) for m in range(3)]
            sb[...] = dot(qkvb[i, 0:PAD, at[0]], qkvb[i, :, at[1]], 1, 1)
            ep[...] = dot(eob[:, at[0]], qkvb[i, :, at[2]], 1, 1)
            s = jnp.where(lane < SEQ, sb[...], NEG)
            e = jnp.exp((s - jnp.max(s, -1, keepdims=True)) * scale)
            probs = e * (1.0 / jnp.sum(e, -1, keepdims=True))
            pb[...] = probs.astype(BF)
            grad = ep[...]
            esb[...] = (
                probs * (grad - jnp.sum(grad * probs, -1, keepdims=True))
            ).astype(BF)
            eub[i, :, at[0]] = (dot(esb[...], qkvb[i, :, at[1]]) * scale).astype(BF)
            eub[i, :, at[1]] = (
                dot(esb[...], qkvb[i, 0:PAD, at[0]], 0, 0)[0:PAD] * scale
            ).astype(BF)
            eub[i, :, at[2]] = dot(pb[...], eob[:, at[0]], 0, 0)[0:PAD].astype(BF)
        tally(layer * 8 + 7, eub[i, :, 0:256].astype(F32), slice(0, 256))
        tally(layer * 8 + 7, eub[i, :, 512:768].astype(F32), slice(512, 768))
        exchange(
            t,
            lambda at: eub[i, at, 0:768],
            lambda c: wa[c * 512 : c * 512 + 512, 0:768],
        )

    order = (5, 4, 3, 2, 1, 0)
    owners_per_block = max(1, 256 // piece_rows)

    def weight_grad(q, lefts, rights, cols):
        slot = q % 4

        def each(b, carry):
            block = pl.ds(pl.multiple_of(b * 256, 256), 256)
            for left, right, at in zip(lefts, rights, cols):
                value = dot(left[0](block), right[0], 0, 0)
                for other, what in zip(left[1:], right[1:]):
                    value = value + dot(other(block), what, 0, 0)
                width = value.shape[1]
                gst[slot, pl.ds(b * owners_per_block, owners_per_block), :, :, at] = (
                    value.astype(BF).reshape(owners_per_block, 2, half_rows, width)
                )
            return carry

        lax.fori_loop(0, D // 256, each, 0)

    def lanes(ref, slot):
        return lambda block: ref[slot, :, block]

    def x_copy(q):
        p = order[q]
        return remote(gst.at[q % 4, :, 1 - dp], xrecv.at[p], gxs.at[p], gxr.at[p], here.x_mate)

    def reduce_start(q):
        x_copy(q).start()

    def z_copy(q, k):
        p = order[q]
        to = here.peer(n, k)
        return remote(
            gst.at[q % 4, to, dp], zrecv.at[p, k], gzs.at[p, k], gzr.at[p, k], {"fsdp": to}
        )

    def reduce_dp(q):
        p = order[q]
        x_copy(q).wait()
        copy = pltpu.make_async_copy(xrecv.at[p], xst, ls.at[60 + p])
        copy.start()
        copy.wait()
        gst[q % 4, :, dp] = (gst[q % 4, :, dp].astype(F32) + xst[...].astype(F32)).astype(BF)

        def each(k, carry):
            z_copy(q, k).start()
            return carry

        lax.fori_loop(1, n, each, 0)

    def reduce_fsdp(q):
        p = order[q]

        def each(k, carry):
            z_copy(q, k).wait()
            return carry

        lax.fori_loop(1, n, each, 0)
        copy = pltpu.make_async_copy(
            zrecv.at[p, pl.ds(1, n - 1)], xst.at[pl.ds(1, n - 1)], ls.at[66 + p]
        )
        copy.start()
        copy.wait()
        total = gst[q % 4, f, dp].astype(F32)
        for k in range(1, n):
            total = total + xst[k].astype(F32)
        fsend[p] = total.astype(BF)
        remote(fsend.at[p], frecv.at[p], gfs.at[p], gfr.at[p], here.x_mate).start()

    def reduce_out(q):
        p = order[q]
        remote(fsend.at[p], frecv.at[p], gfs.at[p], gfr.at[p], here.x_mate).wait()
        need(("gw", q - 1))
        outv[dp] = fsend[p].astype(F32)
        outv[1 - dp] = frecv[p].astype(F32)
        load(("gw", q), outv, gw_all.at[p])

    def grads_hidden(layer, t, q):
        need(("g", 0), ("g", 1))
        weight_grad(
            q,
            [[lanes(eb, t % 4), lanes(eb, (t + 1) % 4)]],
            [[gb[0], gb[1]]],
            [pl.ds(0, D)],
        )
        reduce_start(q)
        need(("n2", 0), ("n2", 1))
        weight_grad(q + 1, [[lanes(nb, 2), lanes(nb, 3)]], [[eub[0], eub[1]]], [pl.ds(0, D)])
        reduce_start(q + 1)

    def grads_attention(layer, t, q):
        need(("n1", 0), ("n1", 1), ("o", 0), ("o", 1))
        weight_grad(
            q,
            [[lanes(nb, 0), lanes(nb, 1)], [lanes(eb, t % 4), lanes(eb, (t + 1) % 4)]],
            [[eub[0, :, 0:768], eub[1, :, 0:768]], [ob[0], ob[1]]],
            [pl.ds(0, 768), pl.ds(768, 256)],
        )
        reduce_start(q)

    hidden(0)
    hidden(1)
    load("wd", w_all.at[2], wd)
    load("wu", w_all.at[1], wu)
    grads_hidden(1, 0, 0)
    load_hidden(0)
    finish(0)
    attention(2)
    finish(1)
    attention(3)
    load("wa", w_all.at[0], wa)
    grads_attention(1, 2, 2)
    load_attention(0)
    finish(2)
    hidden(4)
    reduce_dp(0)
    finish(3)
    hidden(5)
    reduce_dp(1)
    reduce_fsdp(0)
    grads_hidden(0, 4, 3)
    finish(4)
    attention(6)
    finish(5)
    attention(7)
    reduce_dp(2)
    reduce_fsdp(1)
    grads_attention(0, 6, 5)
    finish(6)
    finish(7)
    for t in (8, 9):
        shared(t)
        drop_rows(eb.at[t % 4], cotv.at[t - 8])
        load(("gi", t), cotv.at[t - 8], gi_all.at[t - 8])

    to_core = remote(sm, smc, ks.at[0], kr.at[0], here.core_mate)
    to_core.start()
    reduce_out(0)
    reduce_out(1)
    reduce_dp(3)
    to_core.wait()
    row = lax.rem(lax.broadcasted_iota(jnp.int32, (16, D), 0), 8)
    sm[...] = sm[...] + jnp.where(row < 6, smc[...], 0.0)
    to_x = remote(sm, smx, ks.at[n], kr.at[n], here.x_mate)
    to_x.start()
    reduce_fsdp(2)
    reduce_out(2)
    to_x.wait()
    smz[f] = sm[...] + smx[...]

    def small_copy(k):
        return remote(smz.at[f], smz.at[f], ks.at[k], kr.at[k], {"fsdp": here.peer(n, k)})

    def small_start(k, carry):
        small_copy(k).start()
        return carry

    def small_wait(k, carry):
        source = lax.rem(f + n - k, n)
        remote(smz.at[f], smz.at[source], ks.at[k], kr.at[k], {"fsdp": source}).wait_recv()
        small_copy(k).wait_send()
        return carry

    lax.fori_loop(1, n, small_start, 0)
    reduce_dp(4)
    reduce_fsdp(3)
    reduce_out(3)
    lax.fori_loop(1, n, small_wait, 0)
    total = smz[0]
    for k in range(1, n):
        total = total + smz[k]
    smc[...] = total
    load("small", smc, small_all)
    reduce_dp(5)
    reduce_fsdp(4)
    reduce_out(4)
    reduce_fsdp(5)
    reduce_out(5)
    for name in list(flying):
        need(name)


def backward(n, cot, kept):
    w_all, n_all, qkv_all, o_all, g_all, gp_all, r_all, prm_all = kept
    pieces = w_all.shape[0]
    rows = D // n
    half = rows // 2
    sds = jax.ShapeDtypeStruct
    dma = pltpu.SemaphoreType.DMA
    vm = pltpu.VMEM
    return pl.pallas_call(
        lambda *refs: backward_kernel(n, *refs),
        out_shape=(
            sds((2, SEQ, D), BF),
            sds((pieces, 2, half, D), F32),
            sds((16, D), F32),
            sds((pieces, n, half, D), BF),
            sds((pieces, n, half, D), BF),
        ),
        in_specs=[ANY] * 8 + [pl.BlockSpec(memory_space=pltpu.VMEM)],
        out_specs=[ANY] * 5,
        scratch_shapes=[
            vm((2, SEQ, D), BF),
            vm((D, D), BF),
            vm((D, D), BF),
            vm((D, D), BF),
            vm((4, PAD, D), BF),
            vm((2, HALF, D), F32),
            vm((2, HALF, D), F32),
            vm((2, PAD, D), BF),
            vm((2, PAD, D), BF),
            vm((4, PAD, D), BF),
            vm((2, KEYS, 768), BF),
            vm((2, PAD, 256), BF),
            vm((2, PAD, D), BF),
            vm((2, HALF, D), BF),
            vm((4, HALF, D), BF),
            vm((2, HALF, D), BF),
            vm((HALF, D), F32),
            vm((2, HALF, D), BF),
            vm((PAD, KEYS), F32),
            vm((PAD, KEYS), F32),
            vm((PAD, KEYS), BF),
            vm((PAD, KEYS), BF),
            vm((PAD, 256), BF),
            vm((4, n, 2, half, D), BF),
            vm((n, half, D), BF),
            vm((pieces, half, D), BF),
            vm((pieces, half, D), BF),
            vm((2, half, D), F32),
            vm((16, D), F32),
            vm((16, D), F32),
            vm((16, D), F32),
            vm((n, 16, D), F32),
            dma((8,)),
            dma((8,)),
            dma((8,)),
            dma((8,)),
            dma((10,)),
            dma((10,)),
            dma((72,)),
            dma((pieces,)),
            dma((pieces,)),
            dma((pieces, n)),
            dma((pieces, n)),
            dma((pieces,)),
            dma((pieces,)),
            dma((n + 1,)),
            dma((n + 1,)),
        ],
        compiler_params=pltpu.CompilerParams(
            collective_id=1, has_side_effects=True, vmem_limit_bytes=62 << 20
        ),
        name="backward",
    )(cot, w_all, n_all, qkv_all, o_all, g_all, gp_all, r_all, prm_all)


def on_device(
    images,
    cotangent,
    qkv_weight,
    out_weight,
    up_weight,
    down_weight,
    query_bias,
    value_bias,
    up_bias,
    norm_gain,
    norm_shift,
):
    n = lax.axis_size("fsdp")
    f = lax.axis_index("fsdp")
    wsh = pack_weights(qkv_weight, out_weight, up_weight, down_weight)
    pk = pack_small(n, query_bias, value_bias, up_bias, norm_gain, norm_shift)
    *kept, out_images = forward(n, images, wsh, pk)
    grad_images, gw, small, _, _ = backward(n, cotangent, kept)
    layers = qkv_weight.shape[0]
    gw = gw.reshape(layers, 3, D // n, D)
    grad_qkv = jnp.stack([gw[:, 0, :, 256 * m : 256 * m + 256] for m in range(3)], 1)
    grad_out = gw[:, 0, :, 768:].transpose(0, 2, 1)
    grad_up = gw[:, 1]
    grad_down = gw[:, 2].transpose(0, 2, 1)
    small = small.reshape(layers, 8, D)

    def owned(rows, like):
        whole = rows.reshape(like.shape[:-1] + (n, like.shape[-1]))
        return lax.dynamic_index_in_dim(whole, f, len(like.shape) - 1, keepdims=False)

    grad_gain = owned(jnp.stack([small[:, 0], small[:, 3]], 1), norm_gain)
    grad_shift = owned(
        jnp.stack([small[:, 1], small[:, 4], small[:, 2], small[:, 5]], 1), norm_shift
    )
    grad_query = owned(small[:, 7, 0:256], query_bias)
    grad_value = owned(small[:, 7, 512:768], value_bias)
    grad_upb = owned(small[:, 6], up_bias)
    return (
        out_images,
        grad_images,
        grad_qkv,
        grad_out,
        grad_up,
        grad_down,
        grad_query,
        grad_value,
        grad_upb,
        grad_gain,
        grad_shift,
    )


def solution(mesh):
    specs = (
        P(("dp", "fsdp"), None, None),
        P(("dp", "fsdp"), None, None),
        P(None, None, "fsdp", "tensor"),
        P(None, "tensor", "fsdp"),
        P(None, "fsdp", "tensor"),
        P(None, "tensor", "fsdp"),
        P(None, "tensor", "fsdp"),
        P(None, "tensor", "fsdp"),
        P(None, "tensor", "fsdp"),
        P(None, None, "fsdp"),
        P(None, None, "fsdp"),
    )
    return jax.shard_map(
        on_device, mesh=mesh, in_specs=specs, out_specs=specs, check_vma=False
    )
```

```python
import math

import jax
import jax.numpy as jnp
from jax import lax
from jax.experimental import pallas as pl
from jax.experimental.pallas import tpu as pltpu
from jax.sharding import PartitionSpec as P

BF = jnp.bfloat16
F32 = jnp.float32
MESH = pl.DeviceIdType.MESH
ANY = pl.BlockSpec(memory_space=pl.ANY)
EPSILON = 1e-06
HD = 64
SEQ = 577
PAD = 608
HALF = PAD // 2
KEYS = 640
NEG = -1e30
D = 1024
WIDE = 512


def dot(a, b, ca=1, cb=0):
    return lax.dot_general(a, b, (((ca,), (cb,)), ((), ())), preferred_element_type=F32)


def rows16(i, size=16):
    return pl.ds(pl.multiple_of(i * size, size), size)


def remote(src, dst, ssem, rsem, where):
    return pltpu.make_async_remote_copy(
        src_ref=src,
        dst_ref=dst,
        send_sem=ssem,
        recv_sem=rsem,
        device_id=where,
        device_id_type=MESH,
    )


class Here:
    def __init__(self):
        self.dp = lax.axis_index("dp")
        self.f = lax.axis_index("fsdp")
        t = lax.axis_index("tensor")
        self.core = lax.rem(t, 2)
        self.y = lax.div(t, 2)
        self.core_mate = {"tensor": self.y * 2 + (1 - self.core)}
        self.y_mate = {"tensor": (1 - self.y) * 2 + self.core}
        self.x_mate = {"dp": 1 - self.dp}
        self.own = pl.ds(pl.multiple_of(self.core * HALF, 16), HALF)
        self.mate = pl.ds(pl.multiple_of((1 - self.core) * HALF, 16), HALF)

    def peer(self, n, k):
        return lax.rem(self.f + k, n)

    def greet(self, n):
        barrier = pltpu.get_barrier_semaphore()
        for where in (self.core_mate, self.y_mate, self.x_mate):
            pl.semaphore_signal(barrier, inc=1, device_id=where, device_id_type=MESH)

        def each(k, carry):
            pl.semaphore_signal(
                barrier, inc=1, device_id={"fsdp": self.peer(n, k)}, device_id_type=MESH
            )
            return carry

        lax.fori_loop(1, n, each, 0)
        pl.semaphore_wait(barrier, n + 2)


def standardize(v):
    centered = v - jnp.sum(v, -1, keepdims=True) * (1.0 / D)
    inverse = lax.rsqrt(jnp.sum(centered * centered, -1, keepdims=True) * (1.0 / D) + EPSILON)
    return centered * inverse, inverse


def take_rows(here, whole, half):
    full = (SEQ - HALF) // 16

    def copy(k, carry):
        there = pl.ds(pl.multiple_of(here.core * HALF + k * 16, 16), 16)
        half[rows16(k), :] = whole[there, :].astype(F32)
        return carry

    lax.fori_loop(0, full, copy, 0)

    @pl.when(here.core == 0)
    def _():
        half[full * 16 : HALF, :] = whole[full * 16 : HALF, :].astype(F32)

    @pl.when(here.core == 1)
    def _():
        half[full * 16 : HALF, :] = jnp.zeros((HALF - full * 16, D), F32)
        half[full * 16 : full * 16 + 1, :] = whole[SEQ - 1 : SEQ, :].astype(F32)


def drop_rows(padded, whole):
    def copy(k, carry):
        whole[rows16(k), :] = padded[rows16(k), :]
        return carry

    lax.fori_loop(0, SEQ // 16, copy, 0)
    whole[SEQ - 1 : SEQ, :] = padded[SEQ - 1 : SEQ, :]


XCOLS = 640
SCHEDULE = (
    ("hop", 0, 0), ("pro", 0), ("ln", 0), ("ln", 1), ("hop", 0, 1), ("hop", 1, 0), ("cot", 0),
    ("cot", 1), ("hop", 0, 2), ("hop", 1, 1), ("hop", 0, 3), ("hop", 2, 0), ("hop", 1, 2),
    ("take", 0), ("hop", 2, 1), ("hop", 1, 3), ("hop", 3, 0), ("hop", 2, 2), ("take", 1),
    ("qkv", 0), ("hd", 0, 0), ("hop", 2, 3), ("hop", 3, 1), ("hop", 4, 0), ("hd", 0, 1),
    ("hd", 0, 2), ("hd", 0, 3), ("ex1", 0), ("qkv", 1), ("hop", 3, 2), ("take", 2), ("ex2", 0),
    ("hd", 1, 0), ("hd", 1, 1), ("hd", 1, 2), ("hop", 3, 3), ("hop", 4, 1), ("hop", 5, 0),
    ("hd", 1, 3), ("ex1", 1), ("ex2", 1), ("hop", 4, 2), ("take", 3), ("hop", 4, 3),
    ("hop", 6, 0), ("hop", 5, 1), ("fin", 0), ("take", 4), ("hop", 5, 2), ("hid", 2, 0),
    ("hop", 5, 3), ("hop", 6, 1), ("hop", 7, 0), ("hid", 2, 1), ("hop", 6, 2), ("take", 5),
    ("ex1", 2), ("hop", 7, 1), ("hop", 6, 3), ("hop", 8, 0), ("fin", 1), ("ex2", 2),
    ("hid", 3, 0), ("hop", 7, 2), ("hid", 3, 1), ("ex1", 3), ("hop", 7, 3), ("hop", 8, 1),
    ("hop", 9, 0), ("take", 6), ("ex2", 3), ("hop", 8, 2), ("take", 7), ("hop", 9, 1),
    ("hop", 8, 3), ("hop", 10, 0), ("fin", 2), ("qkv", 4), ("hop", 9, 2), ("hd", 4, 0),
    ("hd", 4, 1), ("hd", 4, 2), ("hd", 4, 3), ("ex1", 4), ("hop", 9, 3), ("hop", 10, 1),
    ("hop", 11, 0), ("take", 8), ("ex2", 4), ("hop", 10, 2), ("take", 9), ("fin", 3),
    ("qkv", 5), ("hop", 10, 3), ("hop", 11, 1), ("hd", 5, 0), ("hd", 5, 1), ("hd", 5, 2),
    ("hd", 5, 3), ("ex1", 5), ("take", 10), ("hop", 11, 2), ("hop", 11, 3), ("ex2", 5),
    ("fin", 4), ("hid", 6, 0), ("hid", 6, 1), ("take", 11), ("ex1", 6), ("ex2", 6), ("fin", 5),
    ("hid", 7, 0), ("hid", 7, 1), ("ex1", 7), ("hb", 8, 0), ("hb", 8, 1), ("ex2", 7),
    ("ex1", 8), ("hb", 9, 0), ("hb", 9, 1), ("ex2", 8), ("ex1", 9), ("g", 0, 0), ("g", 0, 1),
    ("gx", 0), ("rs", 0), ("g", 1, 0), ("g", 1, 1), ("gx", 1), ("rs", 1), ("fin", 6),
    ("ex2", 9), ("fin", 7), ("cz", 0, 1), ("put", 8), ("put", 9), ("cz", 1, 1), ("cz", 0, 2),
    ("cz", 1, 2), ("dpl", 0), ("dps", 0), ("fin", 8), ("cz", 0, 3), ("eo", 10), ("hbk", 10, 0),
    ("hbk", 10, 1), ("cz", 1, 3), ("hbk", 10, 2), ("cx", 0, 1), ("hbk", 10, 3), ("ex1", 10),
    ("dpl", 1), ("fin", 9), ("cx", 0, 2), ("ex2", 10), ("dps", 1), ("eo", 11), ("hbk", 11, 0),
    ("hbk", 11, 1), ("cx", 1, 1), ("hbk", 11, 2), ("hbk", 11, 3), ("cx", 0, 3), ("ex1", 11),
    ("cx", 1, 2), ("cr", 0), ("g", 2, 0), ("ex2", 11), ("g", 2, 1), ("gx", 2), ("rs", 2),
    ("enl", 0), ("fin", 10), ("end", 0), ("cz", 2, 1), ("cx", 1, 3), ("cr", 1), ("hb", 12, 0),
    ("hb", 12, 1), ("ex1", 12), ("cz", 2, 2), ("ex2", 12), ("fin", 11), ("dpl", 2), ("g", 3, 0),
    ("dps", 2), ("cz", 2, 3), ("g", 3, 1), ("cx", 2, 1), ("gx", 3), ("rs", 3), ("hb", 13, 0),
    ("hb", 13, 1), ("ex1", 13), ("cx", 2, 2), ("enl", 1), ("fin", 12), ("cz", 3, 1), ("end", 1),
    ("ex2", 13), ("g", 4, 0), ("g", 4, 1), ("gx", 4), ("eo", 14), ("cx", 2, 3), ("cr", 2),
    ("cz", 3, 2), ("hbk", 14, 0), ("hbk", 14, 1), ("dpl", 3), ("hbk", 14, 2), ("rs", 4),
    ("dps", 3), ("hbk", 14, 3), ("cz", 4, 1), ("ex1", 14), ("cz", 3, 3), ("fin", 13),
    ("cx", 3, 1), ("ex2", 14), ("cz", 4, 2), ("eo", 15), ("hbk", 15, 0), ("dpl", 4),
    ("hbk", 15, 1), ("cx", 3, 2), ("dps", 4), ("hbk", 15, 2), ("hbk", 15, 3), ("ex1", 15),
    ("enl", 2), ("cz", 4, 3), ("end", 2), ("g", 5, 0), ("cx", 3, 3), ("cx", 4, 1), ("cr", 3),
    ("g", 5, 1), ("gx", 5), ("ex2", 15), ("fin", 14), ("enl", 3), ("cx", 4, 2), ("end", 3),
    ("rs", 5), ("put", 16), ("cz", 5, 1), ("cz", 5, 2), ("cx", 4, 3), ("cr", 4), ("dpl", 5),
    ("fin", 15), ("dps", 5), ("cx", 5, 1), ("sm", 0), ("enl", 4), ("put", 17), ("sm", 1),
    ("end", 4), ("cx", 5, 2), ("cz", 5, 3), ("sm", 2), ("cx", 5, 3), ("cr", 5), ("sm", 3),
    ("enl", 5), ("end", 5),
)
ORDER = (5, 4, 3, 2, 1, 0)


def train_kernel(
    n,
    img,
    cot,
    qkv_w,
    out_w,
    up_w,
    down_w,
    pk,
    out_all,
    gi_all,
    gqkv,
    gout,
    gup,
    gdown,
    small_all,
    w_all,
    n_all,
    qkv_all,
    o_all,
    g_all,
    gp_all,
    r_all,
    xrecv,
    frecv,
    pix,
    wa,
    wu,
    wd,
    nb,
    eb,
    rb,
    er,
    gb,
    gpb,
    qkvb,
    ob,
    eub,
    ysend,
    yrecv,
    psend,
    precv,
    sb,
    ep,
    pb,
    esb,
    eob,
    gst,
    xst,
    zrx,
    zrz,
    finx,
    finz,
    outv,
    pkr,
    prm,
    sm,
    smc,
    smx,
    smz,
    zs,
    zr,
    xs,
    xr,
    ks,
    kr,
    ys,
    yr,
    ps,
    pr,
    cs,
    cr,
    ls,
    gxs,
    gxr,
    gzs,
    gzr,
    gfs,
    gfr,
    qs,
    qr,
    credit,
):
    here = Here()
    f, dp = here.f, here.dp
    pieces = w_all.shape[0]
    piece_rows = D // n
    half_rows = piece_rows // 2
    units = 2 * pieces
    scale = 1.0 / math.sqrt(HD)
    here.greet(n)

    flying = {}
    count = [0]

    def load(name, src, dst):
        copy = pltpu.make_async_copy(src, dst, ls.at[count[0]])
        count[0] += 1
        copy.start()
        flying[name] = copy

    def need(*names):
        for name in names:
            if name in flying:
                flying.pop(name).wait()

    pkr[f] = pk[...]

    def small_param(k):
        return remote(pk, pkr.at[f], qs.at[k], qr.at[k], {"fsdp": here.peer(n, k)})

    def param_start(k, carry):
        small_param(k).start()
        return carry

    def param_wait(k, carry):
        source = lax.rem(f + n - k, n)
        remote(pk, pkr.at[source], qs.at[k], qr.at[k], {"fsdp": source}).wait_recv()
        small_param(k).wait_send()
        return carry

    lax.fori_loop(1, n, param_start, 0)

    def place(u, shard, half):
        return w_all.at[
            u // 2,
            pl.ds(pl.multiple_of(shard * piece_rows + half * half_rows, half_rows), half_rows),
            pl.ds((u % 2) * WIDE, WIDE),
        ]

    def ahead(way):
        return {"fsdp": jnp.clip(f + (1 if way == 0 else -1), 0, n - 1)}

    def behind(way):
        return {"fsdp": jnp.clip(f + (-1 if way == 0 else 1), 0, n - 1)}

    def arrives(way, j):
        return (f >= j) if way == 0 else (f + j <= n - 1)

    def leaves(way, j):
        more = (f < n - 1) if way == 0 else (f > 0)
        return jnp.logical_and(more, arrives(way, j))

    def shard_of(way, j):
        return jnp.clip(f - j if way == 0 else f + j, 0, n - 1)

    def z_copy(u, way, j):
        at = place(u, shard_of(way, j), dp)
        return remote(at, at, zs.at[way, u, j], zr.at[way, u, j + 1], ahead(way))

    def x_copy(u, way, j):
        at = place(u, shard_of(way, j), dp)
        return remote(at, at, xs.at[way, u, j], xr.at[way, u, j], here.x_mate)

    def hop(u, j, first=False, last=False):
        if first:
            need(*[("own", u, k) for k in (0, 1)])
        for way in (0, 1):
            if not first:

                @pl.when(arrives(way, j))
                def _():
                    at = place(u, shard_of(way, j), dp)
                    remote(at, at, zs.at[way, u, j], zr.at[way, u, j], ahead(way)).wait_recv()

            if not last:

                @pl.when(leaves(way, j))
                def _():
                    z_copy(u, way, j).start()

            if not first:

                @pl.when(arrives(way, j))
                def _():
                    x_copy(u, way, j).start()

    def travel(u):
        hop(u, 0, first=True)

        def each(j, carry):
            hop(u, j)
            return carry

        lax.fori_loop(1, n - 1, each, 0)
        hop(u, n - 1, last=True)

    def hop_task(u, j):
        if n == 4:
            hop(u, j, first=j == 0, last=j == n - 1)
        elif j == 3:
            travel(u)

    def own_copy(u):
        layer, kind, at = u // 6, (u // 2) % 3, u % 2
        rows = pl.ds(pl.multiple_of(f * piece_rows, piece_rows), piece_rows)
        if kind == 0:
            halves = (qkv_w.at[layer, 2 * at], out_w.at[layer] if at else qkv_w.at[layer, 1])
            for k in (0, 1):
                cols = pl.ds(at * WIDE + k * 256, 256)
                load(("own", u, k), halves[k], w_all.at[u // 2, rows, cols])
        else:
            cols = pl.ds(at * WIDE, WIDE)
            src = (up_w, down_w)[kind - 1].at[layer, :, cols]
            load(("own", u, 0), src, w_all.at[u // 2, rows, cols])

    for u in range(units):
        own_copy(u)

    def take(u):
        def each(j, carry):
            for way in (0, 1):

                @pl.when(arrives(way, j))
                def _():
                    at = place(u, shard_of(way, j), 1 - dp)
                    remote(at, at, xs.at[way, u, j], xr.at[way, u, j], here.x_mate).wait_recv()

            return carry

        lax.fori_loop(1, n, each, 0)
        name, buffer = (("wa", wa), ("wu", wu), ("wd", wd))[(u // 2) % 3]
        cols = pl.ds((u % 2) * WIDE, WIDE)
        load((name, u % 2), w_all.at[u // 2, :, cols], buffer.at[:, cols])

    def weights_sent():
        for u in range(units):

            def each(j, carry):
                for way in (0, 1):

                    @pl.when(leaves(way, j))
                    def _():
                        z_copy(u, way, j).wait_send()

                    @pl.when(jnp.logical_and(j > 0, arrives(way, j)))
                    def _():
                        x_copy(u, way, j).wait_send()

                return carry

            lax.fori_loop(0, n, each, 0)

    def prologue():
        for i in (0, 1):
            load(("pix", i), img.at[i], pix.at[i])
            qkvb[i, PAD:KEYS, :] = jnp.zeros((KEYS - PAD, 768), BF)
        sm[...] = jnp.zeros_like(sm)
        lax.fori_loop(1, n, param_wait, 0)
        total = pkr[0].astype(F32)
        for k in range(1, n):
            total = total + pkr[k].astype(F32)
        prm[...] = total

    def tally(row, value, cols=slice(0, D)):
        sm[row : row + 1, cols] = sm[row : row + 1, cols] + jnp.sum(value, 0, keepdims=True)

    pending = {}

    def share(t, buffer):
        at = buffer.at[t % 4, here.own]
        copy = remote(at, at, cs.at[t], cr.at[t], here.core_mate)
        copy.start()
        pending[t] = copy

    def shared(t):
        if t in pending:
            pending.pop(t).wait()

    def partial_of(t):
        i = t % 2
        if t in (0, 1, 4, 5):
            return (lambda at: ob[i, at, :]), (lambda rows: wa[rows, 768:1024])
        if t in (2, 3, 6, 7):
            need(("wd", 0), ("wd", 1))
            return (lambda at: gb[i, at, :]), (lambda rows: wd[rows, :])
        if t in (8, 9, 12, 13):
            need(("wu", 0), ("wu", 1))
            return (lambda at: eub[i, at, :]), (lambda rows: wu[rows, :])
        return (lambda at: eub[i, at, 0:768]), (lambda rows: wa[rows, 0:768])

    def send_half(t):
        slot = t % 2
        left, right = partial_of(t)
        for c in (0, 1):
            cols = slice(c * 512, c * 512 + 512)
            psend[slot, :, cols] = dot(left(here.mate), right(cols), 1, 1).astype(BF)
        copy = remote(psend.at[slot], precv.at[slot], ps.at[t], pr.at[t], here.core_mate)
        copy.start()
        pending[("p", t)] = copy
        for c in (0, 1):
            cols = slice(c * 512, c * 512 + 512)
            (sb, ep)[c][0:HALF, 0:512] = dot(left(here.own), right(cols), 1, 1)

    def add_half(t):
        slot = t % 2
        pending.pop(("p", t)).wait()
        for c in (0, 1):
            cols = slice(c * 512, c * 512 + 512)
            ysend[t % 3, :, cols] = (
                (sb, ep)[c][0:HALF, 0:512] + precv[slot, :, cols].astype(F32)
            ).astype(BF)
        y_copy = remote(ysend.at[t % 3], yrecv.at[t % 5], ys.at[t], yr.at[t], here.y_mate)
        y_copy.start()
        pending[("y", t)] = y_copy
        if t in (10, 11, 14, 15):
            i, layer = t % 2, 1 - (t - 8) // 4
            tally(layer * 8 + 7, eub[i, :, 0:256].astype(F32), slice(0, 256))
            tally(layer * 8 + 7, eub[i, :, 512:768].astype(F32), slice(512, 768))

    def arrived(t):
        pending.pop(("y", t)).wait()
        return ysend[t % 3].astype(F32) + yrecv[t % 5].astype(F32)

    def finish(t):
        i, layer, mlp = t % 2, t // 4, (t // 2) % 2
        last = t >= 6
        total = arrived(t)
        need(("r", i))
        v = rb[i] + (total + prm[layer * 8 + (5 if mlp else 2)][None])
        if last:
            nb[(t + 2) % 4, here.own, :] = v.astype(BF)
        else:
            base = (layer + 1) * 8 if mlp else layer * 8 + 3
            rb[i] = v
            standard, _ = standardize(v)
            nb[(t + 2) % 4, here.own, :] = (
                standard * prm[base][None] + prm[base + 1][None]
            ).astype(BF)
        share(t + 2, nb)
        if t + 2 < 6:
            load(("r", i), rb.at[i], r_all.at[t + 2])

    lane = lax.broadcasted_iota(jnp.int32, (PAD, KEYS), 1)

    def project_in(t):
        i, layer = t % 2, t // 4
        need(("n", t - 2), ("qkv", i), ("o", i))
        shared(t)
        load(("n", t), nb.at[t % 4], n_all.at[t])
        need(("wa", 0))
        acc = dot(nb[t % 4], wa[:, 0:512])
        qkvb[i, 0:PAD, 0:512] = (acc + prm[layer * 8 + 7, 0:512][None]).astype(BF)
        need(("wa", 1))
        acc = dot(nb[t % 4], wa[:, 512:768])
        qkvb[i, 0:PAD, 512:768] = (acc + prm[layer * 8 + 7, 512:768][None]).astype(BF)
        if layer == 0:
            load(("qkv", i), qkvb.at[i, pl.ds(0, PAD)], qkv_all.at[i])

    def head(t, h):
        i, layer = t % 2, t // 4
        at = [slice(256 * m + h * HD, 256 * m + h * HD + HD) for m in range(3)]
        sb[...] = dot(qkvb[i, 0:PAD, at[0]], qkvb[i, :, at[1]], 1, 1)
        s = jnp.where(lane < SEQ, sb[...], NEG)
        e = jnp.exp((s - jnp.max(s, -1, keepdims=True)) * scale)
        pb[...] = e.astype(BF)
        ep[:, 0:128] = jnp.broadcast_to(1.0 / jnp.sum(e, -1, keepdims=True), (PAD, 128))
        ob[i, :, at[0]] = (dot(pb[...], qkvb[i, :, at[2]]) * ep[:, 0:HD]).astype(BF)
        if layer == 0 and h == 3:
            load(("o", i), ob.at[i], o_all.at[i])

    def hidden(t, c):
        i, layer = t % 2, t // 4
        if c == 0:
            need(("n", t - 2), ("g", i), ("gp", i))
            shared(t)
            if layer == 0:
                load(("n", t), nb.at[t % 4], n_all.at[t])
        cols = slice(c * 512, c * 512 + 512)
        need(("wu", c))
        ep[:, 0:512] = dot(nb[t % 4], wu[:, cols])
        u = ep[:, 0:512] + prm[layer * 8 + 6, cols][None]
        phi = 0.5 * (1.0 + lax.erf(u * math.sqrt(0.5)))
        density = jnp.exp(u * u * -0.5) * (1.0 / math.sqrt(2.0 * math.pi))
        gb[i, :, cols] = (u * phi).astype(BF)
        gpb[i, :, cols] = (phi + u * density).astype(BF)
        if layer == 0 and c == 1:
            load(("g", i), gb.at[i], g_all.at[i])
            load(("gp", i), gpb.at[i], gp_all.at[i])

    owners_per_block = max(1, 256 // piece_rows)
    parts = {"x": pl.ds(0, XCOLS), "z": pl.ds(XCOLS, D - XCOLS)}

    def weight_grad(q, part, lefts, rights, cols):
        def each(b, carry):
            block = pl.ds(pl.multiple_of(b * 256, 256), 256)
            for left, right, at in zip(lefts, rights, cols):
                value = dot(left[0](block), right[0](), 0, 0)
                for other, what in zip(left[1:], right[1:]):
                    value = value + dot(other(block), what(), 0, 0)
                gst[q % 3, pl.ds(b * owners_per_block, owners_per_block), :, :, at] = (
                    value.astype(BF).reshape(owners_per_block, 2, half_rows, value.shape[1])
                )
            return carry

        lax.fori_loop(part * 2, part * 2 + 2, each, 0)

    def lanes(ref, slot):
        return lambda block: ref[slot, :, block]

    def whole(ref, *at):
        return lambda: ref[at]

    def gx_copy(q):
        return remote(
            gst.at[q % 3, :, 1 - dp, :, parts["x"]],
            xrecv.at[q],
            gxs.at[q],
            gxr.at[q],
            here.x_mate,
        )

    def block_of(q, owner, part):
        if part == "x":
            return gst.at[q % 3, owner, dp, :, parts["x"]]
        return gst.at[q % 3, owner, :, :, parts["z"]]

    def landing(q, way, s, part):
        return (zrx if part == "x" else zrz).at[q % 2, way, s]

    def chain_owner(way, s):
        return jnp.clip(n - 1 - s + f if way == 0 else f - (n - 1 - s), 0, n - 1)

    def chain_place(way):
        return f if way == 0 else n - 1 - f

    def chain_copy(q, way, s, part):
        k = 0 if part == "x" else 1
        return remote(
            block_of(q, chain_owner(way, s), part),
            landing(q, way, s, part),
            gzs.at[k, way, q, s],
            gzr.at[k, way, q, s],
            ahead(way),
        )

    def chain(q, s, part, first=False, last=False):
        for way in (0, 1):
            at = chain_place(way)
            if not first:

                @pl.when(jnp.logical_and(at >= 1, at <= s))
                def _():
                    chain_copy(q, way, s - 1, part).wait_recv()
                    block = block_of(q, chain_owner(way, s), part)
                    came = landing(q, way, s - 1, part)
                    block[...] = (block[...].astype(F32) + came[...].astype(F32)).astype(BF)

            if not last:

                @pl.when(at <= s)
                def _():
                    chain_copy(q, way, s, part).start()

        if last:
            final_copy(q, part).start()

    def final_copy(q, part):
        k = 0 if part == "x" else 1
        to = frecv.at[q, dp, :, parts["x"]] if part == "x" else frecv.at[q, :, :, parts["z"]]
        return remote(block_of(q, f, part), to, gfs.at[k, q], gfr.at[k, q], here.x_mate)

    def dp_came(q):
        gx_copy(q).wait()
        load("xst", xrecv.at[q], xst)

    def dp_sum(q):
        need("xst")
        at = gst.at[q % 3, :, dp, :, parts["x"]]
        at[...] = (at[...].astype(F32) + xst[...].astype(F32)).astype(BF)
        chain(q, 0, "x", first=True)

    def many(q, part):
        def each(s, carry):
            chain(q, s, part)
            return carry

        lax.fori_loop(1, n - 1, each, 0)
        chain(q, n - 1, part, last=True)

    def reduce_start(q):
        if q >= 2:
            for way in (0, 1):

                @pl.when(chain_place(way) < n - 1)
                def _():
                    pl.semaphore_wait(credit.at[way], 1)

        chain(q, 0, "z", first=True)

    def chain_task(q, s, part):
        if n == 4:
            chain(q, s, part, last=s == n - 1)
        elif s == 3:
            many(q, part)

    def release(q):
        if q <= 3:
            for way in (0, 1):

                @pl.when(chain_place(way) >= 1)
                def _():
                    pl.semaphore_signal(
                        credit.at[way], inc=1, device_id=behind(way), device_id_type=MESH
                    )

    def reduce_came(q):
        for part in ("x", "z"):
            final_copy(q, part).wait_send()
        at = frecv.at[q, 1 - dp, :, parts["x"]]
        remote(at, at, gfs.at[0, q], gfr.at[0, q], here.x_mate).wait_recv()
        load("finx", at, finx)
        at = frecv.at[q, :, :, parts["z"]]
        remote(at, at, gfs.at[1, q], gfr.at[1, q], here.x_mate).wait_recv()
        load("finz", at, finz)

        def sent(s, carry):
            for way in (0, 1):

                @pl.when(chain_place(way) <= s)
                def _():
                    for part in ("x", "z"):
                        chain_copy(q, way, s, part).wait_send()

            return carry

        lax.fori_loop(0, n - 1, sent, 0)

    def reduce_end(q):
        need("finx", "finz", ("gw", 0), ("gw", 1), ("gw", 2), ("gw", 3))
        outv[dp, :, parts["x"]] = gst[q % 3, f, dp, :, parts["x"]].astype(F32)
        outv[1 - dp, :, parts["x"]] = finx[...].astype(F32)
        outv[:, :, parts["z"]] = gst[q % 3, f, :, :, parts["z"]].astype(F32) + finz[
            ...
        ].astype(F32)
        layer, kind = ORDER[q] // 3, ORDER[q] % 3
        if kind == 0:
            for m in range(3):
                load(("gw", m), outv.at[:, :, pl.ds(m * 256, 256)], gqkv.at[layer, m])
            load(("gw", 3), outv.at[:, :, pl.ds(768, 256)], gout.at[layer])
        else:
            load(("gw", 0), outv, (gup, gdown)[kind - 1].at[layer])

    def finish_back(t):
        i, layer, mlp = t % 2, 1 - (t - 8) // 4, 1 - (t // 2) % 2
        e = arrived(t)
        need(("r", i))
        standard, inverse = standardize(rb[i])
        base = layer * 8 + (3 if mlp else 0)
        tally(base, e * standard)
        tally(base + 1, e)
        scaled = e * prm[base : base + 1, :]
        grad = inverse * (
            scaled
            - jnp.sum(scaled, -1, keepdims=True) * (1.0 / D)
            - standard * (jnp.sum(scaled * standard, -1, keepdims=True) * (1.0 / D))
        )
        total = er[i] + grad
        er[i] = total
        eb[(t + 2) % 4, here.own, :] = total.astype(BF)
        share(t + 2, eb)
        if mlp:
            tally(layer * 8 + 2, total)
        elif layer > 0:
            tally((layer - 1) * 8 + 5, total)
        if t + 2 < 16:
            back = t + 2 - 8
            at = (1 - back // 4) * 4 + (2 if (back // 2) % 2 == 0 else 0) + i
            load(("r", i), r_all.at[at], rb.at[i])

    def hidden_back(t, c):
        i, layer = t % 2, 1 - (t - 8) // 4
        if c == 0:
            shared(t)
            need(("wd", 0), ("wd", 1), ("gp", i))
        cols = slice(c * 512, c * 512 + 512)
        eu = (dot(eb[t % 4], wd[:, cols]) * gpb[i, :, cols].astype(F32)).astype(BF)
        eub[i, :, cols] = eu
        tally(layer * 8 + 6, eu.astype(F32), cols)

    def mix_back(t):
        shared(t)
        need(("wa", 0), ("wa", 1), ("qkv", t % 2))
        eob[...] = dot(eb[t % 4], wa[:, 768:1024]).astype(BF)

    def head_back(t, h):
        i = t % 2
        at = [slice(256 * m + h * HD, 256 * m + h * HD + HD) for m in range(3)]
        sb[...] = dot(qkvb[i, 0:PAD, at[0]], qkvb[i, :, at[1]], 1, 1)
        ep[...] = dot(eob[:, at[0]], qkvb[i, :, at[2]], 1, 1)
        s = jnp.where(lane < SEQ, sb[...], NEG)
        e = jnp.exp((s - jnp.max(s, -1, keepdims=True)) * scale)
        probs = e * (1.0 / jnp.sum(e, -1, keepdims=True))
        pb[...] = probs.astype(BF)
        grad = ep[...]
        esb[...] = (probs * (grad - jnp.sum(grad * probs, -1, keepdims=True))).astype(BF)
        eub[i, :, at[0]] = (dot(esb[...], qkvb[i, :, at[1]]) * scale).astype(BF)
        eub[i, :, at[1]] = (
            dot(esb[...], qkvb[i, 0:PAD, at[0]], 0, 0)[0:PAD] * scale
        ).astype(BF)
        eub[i, :, at[2]] = dot(pb[...], eob[:, at[0]], 0, 0)[0:PAD].astype(BF)

    def grad_block(q, part):
        t = (8, 8, 10, 12, 12, 14)[q]
        rows = [lanes(eb, t % 4), lanes(eb, (t + 1) % 4)]
        every = [pl.ds(0, D)]
        if q in (0, 3):
            shared(t)
            shared(t + 1)
            need(("g", 0), ("g", 1))
            weight_grad(q, part, [rows], [[whole(gb, 0), whole(gb, 1)]], every)
        elif q in (1, 4):
            need(("n2", 0), ("n2", 1))
            weight_grad(
                q,
                part,
                [[lanes(nb, 2), lanes(nb, 3)]],
                [[whole(eub, 0), whole(eub, 1)]],
                every,
            )
        else:
            need(("n1", 0), ("n1", 1), ("o", 0), ("o", 1))
            at = slice(None), slice(0, 768)
            weight_grad(
                q,
                part,
                [[lanes(nb, 0), lanes(nb, 1)], rows],
                [[whole(eub, 0, *at), whole(eub, 1, *at)], [whole(ob, 0), whole(ob, 1)]],
                [pl.ds(0, 768), pl.ds(768, 256)],
            )

    def first_norm(i):
        need(("pix", i))
        take_rows(here, pix.at[i], rb.at[i])
        standard, _ = standardize(rb[i])
        nb[i, here.own, :] = (standard * prm[0:1, :] + prm[1:2, :]).astype(BF)
        share(i, nb)
        load(("r", i), rb.at[i], r_all.at[i])
        load(("pix", i), cot.at[i], pix.at[i])

    def cotangent(i):
        need(("pix", i))
        take_rows(here, pix.at[i], er.at[i])
        eb[i, 576:PAD, :] = jnp.zeros((PAD - 576, D), BF)
        eb[i, 0:SEQ, :] = pix[i]
        tally(8 + 5, er[i])

    def put(t):
        buffer = nb if t < 16 else eb
        out = (out_all if t < 16 else gi_all).at[t % 2]
        shared(t)
        need(("pix", t % 2))
        drop_rows(buffer.at[t % 4], pix.at[t % 2])
        load(("pix", t % 2), pix.at[t % 2], out)
        if t < 16:
            load(("n1", t % 2), n_all.at[4 + t % 2], nb.at[t % 2])

    def small_copy(k):
        return remote(smz.at[f], smz.at[f], ks.at[k], kr.at[k], {"fsdp": here.peer(n, k)})

    def small_start(k, carry):
        small_copy(k).start()
        return carry

    def small_wait(k, carry):
        source = lax.rem(f + n - k, n)
        remote(smz.at[f], smz.at[source], ks.at[k], kr.at[k], {"fsdp": source}).wait_recv()
        small_copy(k).wait_send()
        return carry

    def small_sum(k):
        to_core = remote(sm, smc, ks.at[0], kr.at[0], here.core_mate)
        to_x = remote(sm, smx, ks.at[n], kr.at[n], here.x_mate)
        if k == 0:
            to_core.start()
        elif k == 1:
            to_core.wait()
            row = lax.rem(lax.broadcasted_iota(jnp.int32, (16, D), 0), 8)
            sm[...] = sm[...] + jnp.where(row < 6, smc[...], 0.0)
            to_x.start()
        elif k == 2:
            to_x.wait()
            smz[f] = (sm[...] + smx[...]).astype(BF)
            lax.fori_loop(1, n, small_start, 0)
        else:
            lax.fori_loop(1, n, small_wait, 0)
            total = smz[0].astype(F32)
            for m in range(1, n):
                total = total + smz[m].astype(F32)
            smc[...] = total
            load("small", smc, small_all)

    def refill(*wanted):
        def act():
            for name, src, dst in wanted:
                load(name, src, dst)

        return act

    refills = [
        ({("hb", 8, 1), ("hb", 9, 1)}, refill((("wd", 0), w_all.at[2], wd))),
        ({("ex1", 8), ("ex1", 9)}, refill((("wu", 0), w_all.at[1], wu))),
        ({("ex1", 10), ("ex1", 11)}, refill((("wa", 0), w_all.at[0], wa))),
        ({("g", 0, 1)}, refill(*[(("g", i), g_all.at[i], gb.at[i]) for i in (0, 1)])),
        ({("g", 1, 1)}, refill(*[(("n2", i), n_all.at[2 + i], nb.at[2 + i]) for i in (0, 1)])),
        (
            {("g", 2, 1)},
            refill(
                *[(("o", i), o_all.at[i], ob.at[i]) for i in (0, 1)],
                *[(("n1", i), n_all.at[i], nb.at[i]) for i in (0, 1)],
            ),
        ),
    ]
    for i in (0, 1):
        refills.append(({("hb", 8 + i, 1)}, refill((("gp", i), gp_all.at[i], gpb.at[i]))))
        refills.append(
            (
                {("hbk", 10 + i, 3)},
                refill((("qkv", i), qkv_all.at[i], qkvb.at[i, pl.ds(0, PAD)])),
            )
        )

    tasks = {
        "hop": hop_task,
        "take": take,
        "pro": lambda k: prologue(),
        "ln": first_norm,
        "cot": cotangent,
        "qkv": project_in,
        "hd": head,
        "ex1": send_half,
        "ex2": add_half,
        "fin": lambda t: finish(t) if t < 8 else finish_back(t),
        "hid": hidden,
        "hb": hidden_back,
        "eo": mix_back,
        "hbk": head_back,
        "put": put,
        "g": grad_block,
        "gx": lambda q: gx_copy(q).start(),
        "rs": reduce_start,
        "cz": lambda q, s: chain_task(q, s, "z"),
        "dpl": dp_came,
        "dps": dp_sum,
        "cx": lambda q, s: chain_task(q, s, "x"),
        "cr": release,
        "enl": reduce_came,
        "end": reduce_end,
        "sm": small_sum,
    }
    for name, *at in SCHEDULE:
        tasks[name](*at)
        for waiting, act in refills:
            if (name, *at) in waiting:
                waiting.discard((name, *at))
                if not waiting:
                    act()
    weights_sent()
    for name in list(flying):
        need(name)


def train(n, images, cotangent, qkv_w, out_w, up_w, down_w, pk):
    layers = qkv_w.shape[0]
    pieces = 3 * layers
    units = 2 * pieces
    half = D // n // 2
    sds = jax.ShapeDtypeStruct
    dma = pltpu.SemaphoreType.DMA
    vm = pltpu.VMEM
    return pl.pallas_call(
        lambda *refs: train_kernel(n, *refs),
        out_shape=(
            sds((2, SEQ, D), BF),
            sds((2, SEQ, D), BF),
            sds((layers, 3, 2, half, 256), F32),
            sds((layers, 2, half, 256), F32),
            sds((layers, 2, half, D), F32),
            sds((layers, 2, half, D), F32),
            sds((16, D), F32),
            sds((pieces, D, D), BF),
            sds((6, PAD, D), BF),
            sds((2, PAD, 768), BF),
            sds((2, PAD, 256), BF),
            sds((2, PAD, D), BF),
            sds((2, PAD, D), BF),
            sds((6, HALF, D), F32),
            sds((pieces, n, half, XCOLS), BF),
            sds((pieces, 2, half, D), BF),
        ),
        in_specs=[ANY] * 6 + [pl.BlockSpec(memory_space=pltpu.VMEM)],
        out_specs=[ANY] * 16,
        scratch_shapes=[
            vm((2, SEQ, D), BF),
            vm((D, D), BF),
            vm((D, D), BF),
            vm((D, D), BF),
            vm((4, PAD, D), BF),
            vm((4, PAD, D), BF),
            vm((2, HALF, D), F32),
            vm((2, HALF, D), F32),
            vm((2, PAD, D), BF),
            vm((2, PAD, D), BF),
            vm((2, KEYS, 768), BF),
            vm((2, PAD, 256), BF),
            vm((2, PAD, D), BF),
            vm((3, HALF, D), BF),
            vm((5, HALF, D), BF),
            vm((2, HALF, D), BF),
            vm((2, HALF, D), BF),
            vm((PAD, KEYS), F32),
            vm((PAD, KEYS), F32),
            vm((PAD, KEYS), BF),
            vm((PAD, KEYS), BF),
            vm((PAD, 256), BF),
            vm((3, n, 2, half, D), BF),
            vm((n, half, XCOLS), BF),
            vm((2, 2, n - 1, half, XCOLS), BF),
            vm((2, 2, n - 1, 2, half, D - XCOLS), BF),
            vm((half, XCOLS), BF),
            vm((2, half, D - XCOLS), BF),
            vm((2, half, D), F32),
            vm((n, 16, D), BF),
            vm((16, D), F32),
            vm((16, D), F32),
            vm((16, D), F32),
            vm((16, D), F32),
            vm((n, 16, D), BF),
            dma((2, units, n)),
            dma((2, units, n + 1)),
            dma((2, units, n)),
            dma((2, units, n)),
            dma((n + 1,)),
            dma((n + 1,)),
            dma((16,)),
            dma((16,)),
            dma((16,)),
            dma((16,)),
            dma((18,)),
            dma((18,)),
            dma((128,)),
            dma((pieces,)),
            dma((pieces,)),
            dma((2, 2, pieces, n)),
            dma((2, 2, pieces, n)),
            dma((2, pieces)),
            dma((2, pieces)),
            dma((n,)),
            dma((n,)),
            pltpu.SemaphoreType.REGULAR((2,)),
        ],
        compiler_params=pltpu.CompilerParams(
            collective_id=0, has_side_effects=True, vmem_limit_bytes=63 << 20
        ),
        name="train",
    )(images, cotangent, qkv_w, out_w, up_w, down_w, pk)[:7]


def placed(piece, n, f):
    shape = piece.shape[:-1] + (n, piece.shape[-1])
    at = lax.broadcasted_iota(jnp.int32, shape, len(shape) - 2)
    full = jnp.where(at == f, piece[..., None, :], jnp.zeros((), piece.dtype))
    return full.reshape(shape[:-2] + (n * piece.shape[-1],))


def pack_small(n, query_bias, value_bias, up_bias, norm_gain, norm_shift):
    f = lax.axis_index("fsdp")
    layers = query_bias.shape[0]
    gain = placed(norm_gain, n, f)
    shift = placed(norm_shift, n, f)
    query = placed(query_bias, n, f).reshape(layers, -1)
    value = placed(value_bias, n, f).reshape(layers, -1)
    up = placed(up_bias, n, f).reshape(layers, -1)
    zero = jnp.zeros_like(query)
    rows = [
        gain[:, 0],
        shift[:, 0],
        shift[:, 2],
        gain[:, 1],
        shift[:, 1],
        shift[:, 3],
        up,
        jnp.concatenate([query, zero, value, zero], -1),
    ]
    return jnp.stack(rows, 1).reshape(layers * 8, D)


def on_device(
    images,
    cotangent,
    qkv_weight,
    out_weight,
    up_weight,
    down_weight,
    query_bias,
    value_bias,
    up_bias,
    norm_gain,
    norm_shift,
):
    n = lax.axis_size("fsdp")
    f = lax.axis_index("fsdp")
    pk = pack_small(n, query_bias, value_bias, up_bias, norm_gain, norm_shift)
    out_images, grad_images, gqkv, gout, gup, gdown, small = train(
        n,
        images,
        cotangent,
        qkv_weight,
        out_weight.transpose(0, 2, 1),
        up_weight,
        down_weight.transpose(0, 2, 1),
        pk,
    )
    layers = qkv_weight.shape[0]
    grad_qkv = gqkv.reshape(qkv_weight.shape)
    grad_out = gout.reshape(layers, D // n, -1).transpose(0, 2, 1)
    grad_up = gup.reshape(up_weight.shape)
    grad_down = gdown.reshape(layers, D // n, -1).transpose(0, 2, 1)
    small = small.reshape(layers, 8, D)

    def owned(rows, like):
        whole = rows.reshape(like.shape[:-1] + (n, like.shape[-1]))
        return lax.dynamic_index_in_dim(whole, f, len(like.shape) - 1, keepdims=False)

    grad_gain = owned(jnp.stack([small[:, 0], small[:, 3]], 1), norm_gain)
    grad_shift = owned(
        jnp.stack([small[:, 1], small[:, 4], small[:, 2], small[:, 5]], 1), norm_shift
    )
    grad_query = owned(small[:, 7, 0:256], query_bias)
    grad_value = owned(small[:, 7, 512:768], value_bias)
    grad_upb = owned(small[:, 6], up_bias)
    return (
        out_images,
        grad_images,
        grad_qkv,
        grad_out,
        grad_up,
        grad_down,
        grad_query,
        grad_value,
        grad_upb,
        grad_gain,
        grad_shift,
    )


def solution(mesh):
    specs = (
        P(("dp", "fsdp"), None, None),
        P(("dp", "fsdp"), None, None),
        P(None, None, "fsdp", "tensor"),
        P(None, "tensor", "fsdp"),
        P(None, "fsdp", "tensor"),
        P(None, "tensor", "fsdp"),
        P(None, "tensor", "fsdp"),
        P(None, "tensor", "fsdp"),
        P(None, "tensor", "fsdp"),
        P(None, None, "fsdp"),
        P(None, None, "fsdp"),
    )
    return jax.shard_map(
        on_device, mesh=mesh, in_specs=specs, out_specs=specs, check_vma=False
    )
```
